128 devices in a mesh: gz: 8 (over z, core), yx: 16 (over y, x).
Axes of the slice: x: 4, y: 4, z: 4, core: 2. Of those that a mesh axis runs over, the one named last changes fastest.
Arguments:
- features: bfloat16 [12, 4, 256, 2048], P(None, None, 'yx', 'gz'), may hold values from -6 to 6
- conv_weight: bfloat16 [3, 12, 3, 3, 3], replicated, may hold values from -0.3125 to 0.3125
- conv_bias: float32 [3], replicated, may hold values from -3 to 3
- fragments: int32 [4, 256, 2048], P(None, 'yx', 'gz'), may hold values from 1 to 16000, as said below
- pair_slot: int32 [3, 4, 256, 2048], P(None, None, 'yx', 'gz'), may hold values from 0 to 4095
- slot_bucket: int32 [128, 4096], P(('gz', 'yx')), may hold values from 0 to 8191, as said below
- arrival_row: int32 [128, 128, 64], P(('gz', 'yx')), may hold values from 0 to 4095
Outputs:
- affinity: bfloat16 [3, 4, 256, 2048], P(None, None, 'yx', 'gz')
- edge_mean: float32 [524288], P(('gz', 'yx'))
The draws below stay inside these ranges and needn't reach their ends.
Inputs may be any that keep to these rules, and one draw needn't show every extreme that they name: Ids of supervoxel fragments; neighbouring voxels within a slice mostly share an id. `slot_bucket`: each row holds distinct values; row s lists the slots of device s, value // 64 is the slot's owner (its index along gz+yx) and value % 64 its place in the bucket for that owner.
All inputs are finite; a program needn't handle non-finite values.
Results may differ from the reference program's by a relative error of at most 0.005.
Values may be sent and summed in bfloat16 or wider, within the bound.
No kernel may reach another device: no remote copies, remote signals or barrier semaphores. Data moves between devices by JAX's collectives and lax.ppermute only.
A program may use at most 64 MiB of HBM per device.

```python
import jax
import jax.numpy as jnp
from jax import lax

C_IN = 12
C_OUT = 3
Z = 4
YD = 16
XD = 256
BUCKET = 64
E_OWN = 4096
P_LOC = 4096
Y = 256
X = 2048
N_YX = 16
DEVICES = 128


def draw_fragments(key, part):
    first, second, third = jax.random.split(key, 3)
    coarse = jax.random.randint(first, (Z, Y // 8 + 1, X // 8 + 1), 1, 16001)
    jitter_y = jax.random.randint(second, (Z, Y, X), -3, 4)
    jitter_x = jax.random.randint(third, (Z, Y, X), -3, 4)
    row_index = jnp.clip(jnp.arange(Y)[None, :, None] + jitter_y, 0, Y - 1) // 8
    column_index = jnp.clip(jnp.arange(X)[None, None, :] + jitter_x, 0, X - 1) // 8
    layers = jnp.arange(Z)[:, None, None]
    return coarse[layers, row_index, column_index].astype(jnp.int32)


def draw_slot_bucket(key, part):
    first, second = jax.random.split(jax.random.fold_in(key, 7))
    favored = jax.random.randint(first, (), 0, DEVICES)
    orders = jax.vmap(lambda subkey: jax.random.permutation(subkey, DEVICES * BUCKET))(jax.random.split(second, DEVICES))
    owner_of = jnp.arange(DEVICES * BUCKET) // BUCKET
    scores = orders + jnp.where(owner_of == favored, DEVICES * BUCKET, 0)[None, :]
    ranked = jnp.argsort(-scores, axis=1, stable=True)
    return ranked[:, :P_LOC].astype(jnp.int32)


def plant(values, key, low, top_value):
    longest = values.shape.index(max(values.shape))
    spots = []
    for shift in (0, 1):
        where = [jax.random.randint(jax.random.fold_in(key, axis), (), 0, length) for axis, length in enumerate(values.shape)]
        where[longest] = (where[longest] + shift) % values.shape[longest]
        spots.append(tuple(where))
    return values.at[spots[0]].set(low).at[spots[1]].set(top_value)


def block_scale(key, dims, pieces, smallest, largest):
    level, own = 1.0, jax.random.fold_in(key, 6)
    for dim, parts in pieces:
        steps = jnp.exp(jax.random.uniform(jax.random.fold_in(own, dim), (parts,), jnp.float32, smallest / len(pieces), largest / len(pieces)))
        level = level * jnp.repeat(steps, dims[dim] // parts).reshape([-1 if axis == dim else 1 for axis in range(len(dims))])
    return level


def bell_draw(key, shape, width, reach, pieces=(), held_as=jnp.bfloat16):
    array = jax.random.normal(key, shape, jnp.float32) * width
    if len(pieces) > 0:
        array = block_scale(key, shape, pieces, -0.22, 0.18) * array
    return jnp.clip(array, min=-reach, max=reach).astype(held_as)


def setup_inputs(seed: int = 0) -> dict:
    splits = jax.random.split(jax.random.key(seed), 8)
    return {
        "features": bell_draw(splits[0], (C_IN, Z, Y, X), 1.0, 6.0, ((2, 16), (3, 8))),
        "conv_weight": bell_draw(splits[1], (C_OUT, C_IN, 3, 3, 3), (27 * C_IN) ** -0.5, 0.3125),
        "conv_bias": bell_draw(splits[2], (C_OUT,), 1.0, 3.0, (), jnp.float32),
        "fragments": draw_fragments(jax.random.fold_in(splits[7], 71), 0),
        "pair_slot": plant(jax.random.randint(splits[4], (3, Z, Y, X), 0, P_LOC), jax.random.fold_in(splits[4], 1), 0, P_LOC - 1).astype(jnp.int32),
        "slot_bucket": draw_slot_bucket(jax.random.fold_in(splits[7], 71), 0),
        "arrival_row": plant(jax.random.randint(splits[6], (DEVICES, DEVICES, BUCKET), 0, E_OWN), jax.random.fold_in(splits[6], 1), 0, E_OWN - 1).astype(jnp.int32),
    }


def convolve(volume, kernel, padding):
    result = lax.conv_general_dilated(volume[None], kernel, (1, 1, 1), padding, dimension_numbers=("NCDHW", "OIDHW", "NCDHW"), preferred_element_type=jnp.float32)
    return result[0]


def reference(features, conv_weight, conv_bias, fragments, pair_slot, slot_bucket, arrival_row):
    logits = convolve(features, conv_weight, ((1, 1), (1, 1), (1, 1))) + conv_bias[:, None, None, None]
    affinity = jax.nn.sigmoid(logits).astype(jnp.bfloat16)
    depth_ids = lax.broadcasted_iota(jnp.int32, fragments.shape, 0)
    height_ids = lax.broadcasted_iota(jnp.int32, fragments.shape, 1)
    width_ids = lax.broadcasted_iota(jnp.int32, fragments.shape, 2)
    under_z = jnp.concatenate([fragments[:1], fragments[:-1]], axis=0)
    under_y = jnp.concatenate([fragments[:, :1], fragments[:, :-1]], axis=1)
    under_x = jnp.concatenate([fragments[:, :, :1], fragments[:, :, :-1]], axis=2)
    crossing = jnp.stack([(fragments != under_z) & (depth_ids > 0), (fragments != under_y) & (height_ids > 0), (fragments != under_x) & (width_ids > 0)]).astype(jnp.int32)
    device_ids = (width_ids // XD) * N_YX + height_ids // YD
    slot_ids = jnp.where(crossing == 1, pair_slot, P_LOC) + device_ids[None] * (P_LOC + 1)
    values = jnp.where(crossing == 1, affinity.astype(jnp.float32), jnp.float32(0.0))
    tallies = crossing.astype(jnp.float32)
    slot_sums = jax.ops.segment_sum(values.ravel(), slot_ids.ravel(), DEVICES * (P_LOC + 1)).reshape(DEVICES, P_LOC + 1)[:, :P_LOC]
    slot_counts = jax.ops.segment_sum(tallies.ravel(), slot_ids.ravel(), DEVICES * (P_LOC + 1)).reshape(DEVICES, P_LOC + 1)[:, :P_LOC]
    owners = slot_bucket // BUCKET
    places = slot_bucket % BUCKET
    sources = lax.broadcasted_iota(jnp.int32, slot_bucket.shape, 0)
    edge_ids = owners * E_OWN + arrival_row[owners, sources, places]
    edge_sums = jax.ops.segment_sum(slot_sums.ravel(), edge_ids.ravel(), DEVICES * E_OWN)
    edge_counts = jax.ops.segment_sum(slot_counts.ravel(), edge_ids.ravel(), DEVICES * E_OWN)
    edge_mean = edge_sums / jnp.maximum(edge_counts, 1.0)
    return affinity, edge_mean
```

```python
import functools

import jax
import jax.numpy as jnp
from jax import lax
from jax.experimental import pallas as pl
from jax.experimental.pallas import tpu as pltpu
from jax.sharding import PartitionSpec as P

C_IN, C_OUT, Z, YD, XD = 12, 3, 4, 16, 256
BUCKET, E_OWN, P_LOC = 64, 4096, 4096
CZ = C_IN * Z
CELLS = CZ * YD
DEPTH = CELLS + 2 * CZ + 32
WIDE = DEPTH + 2 * Z * YD
ROWS = Z * YD
LANES = 128
HIGH = P_LOC // LANES

f32, bf16, i32 = jnp.float32, jnp.bfloat16, jnp.int32


def iota(shape, dim):
    return lax.broadcasted_iota(i32, shape, dim)


def along(a, b):
    return lax.dot_general(a, b, (((1,), (1,)), ((), ())), preferred_element_type=f32)


def whole(count):
    return [pl.BlockSpec(memory_space=pltpu.VMEM)] * count


def rows_kernel(cells, ids, up, down):
    row = iota((2 * CZ, CELLS), 0)
    wanted = jnp.where(row < CZ, row * YD, (row - CZ) * YD + YD - 1)
    pick = jnp.where(iota((2 * CZ, CELLS), 1) == wanted, 1.0, 0.0).astype(bf16)
    picked = jnp.dot(pick, cells[...], preferred_element_type=f32).astype(bf16)
    up[...] = picked[:CZ]
    down[:CZ] = picked[CZ:]
    last = jnp.concatenate([ids[(z + 1) * YD - 1 : (z + 1) * YD] for z in range(Z)], axis=0)
    pair = jnp.concatenate([last >> 7, last & 127], axis=0)
    down[CZ:] = pair.astype(f32).astype(bf16)


def fill(wide, cells, top, bottom):
    wide[:CELLS] = cells[...]
    wide[CELLS : CELLS + CZ] = top[:CZ]
    wide[CELLS + CZ : CELLS + 2 * CZ] = bottom[...]
    wide[CELLS + 2 * CZ : DEPTH] = jnp.zeros((DEPTH - CELLS - 2 * CZ, XD), bf16)


def columns_kernel(cells, top, bottom, ids, left, right, wide):
    fill(wide, cells, top, bottom)
    wide[DEPTH : DEPTH + ROWS] = (ids[...] >> 7).astype(f32).astype(bf16)
    wide[DEPTH + ROWS :] = (ids[...] & 127).astype(f32).astype(bf16)
    row, lane = iota((8, XD), 0), iota((8, XD), 1)
    pick = jnp.where(lane == jnp.where(row == 0, 0, XD - 1), 1.0, 0.0).astype(bf16)
    picked = along(pick, wide[...])
    left[...] = picked[0:1]
    right[...] = picked[1:2]


def build_taps(weights, taps):
    k = iota((LANES, DEPTH), 1)
    channel = jnp.where(k < CELLS, k // (Z * YD), ((k - CELLS) % CZ) // Z)
    channel = jnp.where(k < CELLS + 2 * CZ, channel, LANES)
    spread = jnp.where(iota((LANES, DEPTH), 0) == channel, 1.0, 0.0).astype(bf16)
    lines = jnp.dot(weights[...], spread, preferred_element_type=f32)
    m, k = iota((ROWS, DEPTH), 0), iota((ROWS, DEPTH), 1)
    inner = k < CELLS
    z_in = jnp.where(inner, (k // YD) % Z, (k - CELLS) % Z)
    y_in = jnp.where(inner, k % YD, jnp.where(k < CELLS + CZ, -1, YD))
    y_in = jnp.where(k < CELLS + 2 * CZ, y_in, 2 * YD)
    dz, dy = z_in - m // YD + 1, y_in - m % YD + 1
    code = jnp.where((dz >= 0) & (dz < 3) & (dy >= 0) & (dy < 3), dz * 3 + dy, -1)
    for block in range(9):
        tap = jnp.zeros((ROWS, DEPTH), f32)
        for ab in range(9):
            line = lines[block * 9 + ab : block * 9 + ab + 1]
            tap = jnp.where(code == ab, line, tap)
        taps[block * ROWS : (block + 1) * ROWS] = tap.astype(bf16)


def one_hot(line, count, value=None):
    hit = iota((count, line.shape[1]), 0) == line
    return jnp.where(hit, 1.0 if value is None else value, 0.0).astype(bf16)


def main_kernel(cells, top, bottom, left, right, ids, slots, bucket, weights, bias, affinity, outgoing, wide, taps, value, cross):
    fill(wide, cells, top, bottom)
    build_taps(weights, taps)
    product = jnp.dot(taps[...], wide[...], preferred_element_type=f32)
    edge_row = iota((8, WIDE), 0)
    edges = jnp.where(edge_row == 0, left[...], jnp.where(edge_row == 1, right[...], 0.0)).astype(bf16)
    outer = along(taps[...], edges[:, :DEPTH])
    part = C_OUT * ROWS
    lane = iota((part, XD), 1)
    logits = product[part : 2 * part]
    logits += jnp.where(lane == 0, outer[:part, 0:1], pltpu.roll(product[:part], 1, 1))
    logits += jnp.where(lane == XD - 1, outer[2 * part :, 1:2], pltpu.roll(product[2 * part :], XD - 1, 1))
    channel = iota((part, XD), 0) // ROWS
    logits += jnp.where(channel == 0, bias[0], jnp.where(channel == 1, bias[1], bias[2]))
    soft = (1.0 / (1.0 + jnp.exp(-logits))).astype(bf16)
    affinity[...] = soft
    soft = soft.astype(f32)

    here = ids[...]
    m, n = iota((ROWS, XD), 0), iota((ROWS, XD), 1)
    under_z = jnp.concatenate([here[:YD], here[:-YD]], axis=0)
    above = top[CZ:].astype(f32)
    above = (above[:Z] * 128.0 + above[Z:]).astype(i32)
    above = jnp.concatenate([jnp.broadcast_to(above[z : z + 1], (YD, XD)) for z in range(Z)], axis=0)
    under_y = jnp.where(m % YD == 0, above, pltpu.roll(here, 1, 0))
    k = iota((ROWS, 2 * ROWS), 1)
    r = iota((ROWS, 2 * ROWS), 0)
    join = jnp.where(k == r, 128.0, jnp.where(k == r + ROWS, 1.0, 0.0)).astype(bf16)
    beside = along(join, edges[:, DEPTH:])[:, 0:1].astype(i32)
    under_x = jnp.where(n == 0, beside, pltpu.roll(here, 1, 1))
    for d, under in enumerate((under_z, under_y, under_x)):
        differs = (here != under) & (under > 0)
        differs = jnp.where(differs, 1.0, 0.0)
        cross[d * ROWS : (d + 1) * ROWS] = differs
        value[d * ROWS : (d + 1) * ROWS] = differs * soft[d * ROWS : (d + 1) * ROWS]

    group = 8

    def step(i, total):
        a_parts, b_parts = [], []
        base = pl.multiple_of(i * group, group)
        slot8, value8, cross8 = slots[pl.ds(base, group)], value[pl.ds(base, group)], cross[pl.ds(base, group)]
        for j in range(group):
            slot = slot8[j : j + 1]
            high, low = slot >> 7, slot & 127
            a_parts.append(
                jnp.concatenate([one_hot(high, HIGH, value8[j : j + 1]), one_hot(high, HIGH, cross8[j : j + 1])], axis=0)
            )
            b_parts.append(one_hot(low, LANES))
        return total + along(jnp.concatenate(a_parts, axis=1), jnp.concatenate(b_parts, axis=1))

    total = lax.fori_loop(0, 3 * ROWS // group, step, jnp.zeros((2 * HIGH, LANES), f32))
    total = total.astype(bf16).astype(f32)

    sent = jnp.zeros((LANES, LANES), f32)
    for h0 in range(0, HIGH, 8):
        a_parts, b_parts = [], []
        for h in range(h0, h0 + 8):
            place = bucket[h : h + 1]
            owner, place = place >> 6, place & 63
            a_parts.append(one_hot(owner, LANES))
            b_parts.append(
                jnp.concatenate(
                    [one_hot(place, BUCKET, total[h : h + 1]), one_hot(place, BUCKET, total[HIGH + h : HIGH + h + 1])],
                    axis=0,
                )
            )
        sent += along(jnp.concatenate(a_parts, axis=1), jnp.concatenate(b_parts, axis=1))
    outgoing[...] = sent.astype(bf16)


def edges_kernel(arrived, rows, mean):
    got = arrived[...].astype(f32)
    half = got.shape[0] // 2
    lane = iota((half, LANES), 1)
    first, second = got[:half], got[half:]
    sums = jnp.where(lane < BUCKET, first, pltpu.roll(second, BUCKET, 1))
    counts = jnp.where(lane < BUCKET, pltpu.roll(first, BUCKET, 1), second)
    targets = jnp.concatenate([rows[:half], rows[half:]], axis=1)
    total = jnp.zeros((2 * HIGH, LANES), f32)
    for h0 in range(0, half, 16):
        a_parts, b_parts = [], []
        for h in range(h0, h0 + 16):
            target = targets[h : h + 1]
            high, low = target >> 7, target & 127
            a_parts.append(
                jnp.concatenate([one_hot(high, HIGH, sums[h : h + 1]), one_hot(high, HIGH, counts[h : h + 1])], axis=0)
            )
            b_parts.append(one_hot(low, LANES))
        total += along(jnp.concatenate(a_parts, axis=1), jnp.concatenate(b_parts, axis=1))
    mean[...] = total[:HIGH] / jnp.maximum(total[HIGH:], 1.0)


def passed(block, axis, distance):
    size = lax.axis_size(axis)
    return lax.ppermute(block, axis, [(i, i + distance) for i in range(size) if 0 <= i + distance < size])


def local(features, conv_weight, conv_bias, fragments, pair_slot, slot_bucket, arrival_row):
    devices = lax.axis_size("gz") * lax.axis_size("yx")
    cells = features.reshape(CELLS, XD)
    ids = fragments.reshape(ROWS, XD)
    slots = pair_slot.reshape(C_OUT * ROWS, XD)
    bucket = slot_bucket.reshape(HIGH, LANES)
    weights = conv_weight.transpose(4, 0, 2, 3, 1).reshape(81, C_IN)
    weights = jnp.pad(weights, ((0, 7), (0, LANES - C_IN)))

    shape = jax.ShapeDtypeStruct
    up, down = pl.pallas_call(
        rows_kernel,
        out_shape=(shape((CZ, XD), bf16), shape((CZ + 2 * Z, XD), bf16)),
        in_specs=whole(2),
        out_specs=tuple(whole(2)),
    )(cells, ids)
    top = passed(down, "yx", 1)
    bottom = passed(up, "yx", -1)
    to_left, to_right = pl.pallas_call(
        columns_kernel,
        out_shape=(shape((1, WIDE), f32), shape((1, WIDE), f32)),
        in_specs=whole(4),
        out_specs=tuple(whole(2)),
        scratch_shapes=[pltpu.VMEM((WIDE, XD), bf16)],
    )(cells, top, bottom, ids)
    left = passed(to_right, "gz", 1)
    right = passed(to_left, "gz", -1)
    affinity, outgoing = pl.pallas_call(
        main_kernel,
        out_shape=(shape((C_OUT * ROWS, XD), bf16), shape((devices, 2 * BUCKET), bf16)),
        in_specs=whole(9) + [pl.BlockSpec(memory_space=pltpu.SMEM)],
        out_specs=tuple(whole(2)),
        scratch_shapes=[
            pltpu.VMEM((DEPTH, XD), bf16),
            pltpu.VMEM((9 * ROWS, DEPTH), bf16),
            pltpu.VMEM((C_OUT * ROWS, XD), f32),
            pltpu.VMEM((C_OUT * ROWS, XD), f32),
        ],
    )(cells, top, bottom, left, right, ids, slots, bucket, weights, conv_bias)
    arrived = lax.all_to_all(outgoing, ("gz", "yx"), split_axis=0, concat_axis=0, tiled=True)
    mean = pl.pallas_call(
        edges_kernel,
        out_shape=shape((HIGH, LANES), f32),
        in_specs=whole(2),
        out_specs=whole(1)[0],
    )(arrived, arrival_row[0])
    return affinity.reshape(C_OUT, Z, YD, XD), mean.reshape(E_OWN)


def solution(mesh):
    return jax.shard_map(
        local,
        mesh=mesh,
        in_specs=(
            P(None, None, "yx", "gz"),
            P(),
            P(),
            P(None, "yx", "gz"),
            P(None, None, "yx", "gz"),
            P(("gz", "yx"), None),
            P(("gz", "yx"), None, None),
        ),
        out_specs=(P(None, None, "yx", "gz"), P(("gz", "yx"))),
        check_vma=False,
    )
```

```python
import functools

import jax
import jax.numpy as jnp
from jax import lax
from jax.experimental import pallas as pl
from jax.experimental.pallas import tpu as pltpu
from jax.sharding import PartitionSpec as P

C_IN, C_OUT, Z, YD, XD = 12, 3, 4, 16, 256
BUCKET, E_OWN, P_LOC = 64, 4096, 4096
CZ = C_IN * Z
CELLS = CZ * YD
DEPTH = CELLS + 2 * CZ + 32
WIDE = DEPTH + 2 * Z * YD
ROWS = Z * YD
LANES = 128
HIGH = P_LOC // LANES

TAP_ROWS = 9 * ROWS
PART = C_OUT * ROWS

f32, bf16, i32 = jnp.float32, jnp.bfloat16, jnp.int32


def iota(shape, dim):
    return lax.broadcasted_iota(i32, shape, dim)


def along(a, b):
    return lax.dot_general(a, b, (((1,), (1,)), ((), ())), preferred_element_type=f32)


def whole(count):
    return [pl.BlockSpec(memory_space=pltpu.VMEM)] * count


def near(shape, dtype):
    return pltpu.VMEM(shape, dtype)


def held(x):
    return pltpu.with_memory_space_constraint(x, pltpu.VMEM)


def rows_kernel(cells, ids, up, down):
    row = iota((2 * CZ, CELLS), 0)
    wanted = jnp.where(row < CZ, row * YD, (row - CZ) * YD + YD - 1)
    pick = jnp.where(iota((2 * CZ, CELLS), 1) == wanted, 1.0, 0.0).astype(bf16)
    picked = jnp.dot(pick, cells[...], preferred_element_type=f32).astype(bf16)
    up[...] = picked[:CZ]
    down[:CZ] = picked[CZ:]
    last = jnp.concatenate([ids[(z + 1) * YD - 1 : (z + 1) * YD] for z in range(Z)], axis=0)
    pair = jnp.concatenate([last >> 7, last & 127], axis=0)
    down[CZ:] = pair.astype(f32).astype(bf16)


def pick_ends():
    row, lane = iota((8, XD), 0), iota((8, XD), 1)
    return jnp.where((row < 2) & (lane == row * (XD - 1)), 1.0, 0.0).astype(bf16)


def columns_kernel(cells, top, bottom, ids, after, left, right, wide):
    wide[:CELLS] = cells[...]
    wide[CELLS : CELLS + CZ] = top[:CZ]
    wide[CELLS + CZ : CELLS + 2 * CZ] = bottom[...]
    wide[CELLS + 2 * CZ : DEPTH] = jnp.zeros((DEPTH - CELLS - 2 * CZ, XD), bf16)
    wide[DEPTH : DEPTH + ROWS] = (ids[...] >> 7).astype(f32).astype(bf16)
    wide[DEPTH + ROWS :] = (ids[...] & 127).astype(f32).astype(bf16)
    picked = along(pick_ends(), wide[...])
    left[...] = picked[0:1]
    right[...] = picked[1:2]


def taps_kernel(cells, weights, bias, taps, logits, flat):
    flat[...] = jnp.zeros(flat.shape, f32)
    for i in range(27):
        flat[8 * i : 8 * i + 3, :C_IN] = weights[i].astype(f32)
    k = iota((LANES, DEPTH), 1)
    channel = jnp.where(k < CELLS, k // (Z * YD), ((k - CELLS) % CZ) // Z)
    channel = jnp.where(k < CELLS + 2 * CZ, channel, LANES)
    spread = jnp.where(iota((LANES, DEPTH), 0) == channel, 1.0, 0.0).astype(bf16)
    lines = jnp.dot(flat[...].astype(bf16), spread, preferred_element_type=f32)
    for t in range(DEPTH // LANES):
        y, k = iota((YD, LANES), 0), iota((YD, LANES), 1) + t * LANES
        inner = k < CELLS
        z_in = jnp.where(inner, (k // YD) % Z, (k - CELLS) % Z)
        y_in = jnp.where(inner, k % YD, jnp.where(k < CELLS + CZ, -1, YD))
        y_in = jnp.where(k < CELLS + 2 * CZ, y_in, 3 * YD)
        dy = y_in - y + 1
        for e in range(3):
            for o in range(C_OUT):
                bands = []
                for a in range(3):
                    band = jnp.zeros((YD, LANES), f32)
                    for b in range(3):
                        r = (o * 9 + a * 3 + b) * 8 + e
                        band = jnp.where(dy == b, lines[r : r + 1, t * LANES : (t + 1) * LANES], band)
                    bands.append(band)
                for z in range(Z):
                    tap = jnp.zeros((YD, LANES), f32)
                    for a in range(3):
                        if 0 <= z + a - 1 < Z:
                            tap = jnp.where(z_in == z + a - 1, bands[a], tap)
                    row = ((e * C_OUT + o) * Z + z) * YD
                    taps[row : row + YD, t * LANES : (t + 1) * LANES] = tap.astype(bf16)
    product = jnp.dot(taps[:, :CELLS], cells[...], preferred_element_type=f32)
    channel = iota((PART, XD), 0) // ROWS
    bias = jnp.where(channel == 0, bias[0], jnp.where(channel == 1, bias[1], bias[2]))
    logits[...] = shifted(product) + bias


def shifted(product):
    lane = iota((PART, XD), 1)
    total = product[PART : 2 * PART]
    total += jnp.where(lane == 0, 0.0, pltpu.roll(product[:PART], 1, 1))
    return total + jnp.where(lane == XD - 1, 0.0, pltpu.roll(product[2 * PART :], XD - 1, 1))


def sigmoid(x):
    return (1.0 / (1.0 + jnp.exp(-x))).astype(bf16)


def one_hot(line, count, value=None):
    hit = iota((count, line.shape[1]), 0) == line
    return jnp.where(hit, 1.0 if value is None else value, 0.0).astype(bf16)


def pair_hot(line, count, first, second):
    return jnp.concatenate([one_hot(line, count, first), one_hot(line, count, second)], axis=0)


def inner_kernel(taps, logits, top, bottom, ids, slots, full, sums, ends, halo, value, cross):
    halo[:CZ] = top[:CZ]
    halo[CZ : 2 * CZ] = bottom[...]
    halo[2 * CZ :] = jnp.zeros((LANES - 2 * CZ, XD), bf16)
    total = logits[...] + shifted(jnp.dot(taps[:, CELLS:], halo[...], preferred_element_type=f32))
    full[...] = total
    soft = sigmoid(total).astype(f32)

    here = ids[...]
    m, n = iota((ROWS, XD), 0), iota((ROWS, XD), 1)
    under_z = jnp.concatenate([here[:YD], here[:-YD]], axis=0)
    above = top[CZ:].astype(f32)
    above = (above[:Z] * 128.0 + above[Z:]).astype(i32)
    above = jnp.concatenate([jnp.broadcast_to(above[z : z + 1], (YD, XD)) for z in range(Z)], axis=0)
    under_y = jnp.where(m % YD == 0, above, pltpu.roll(here, 1, 0))
    under_x = jnp.where(n == 0, here, pltpu.roll(here, 1, 1))
    inside = (n > 0) & (n < XD - 1)
    whole_cross = []
    for d, under in enumerate((under_z, under_y, under_x)):
        differs = jnp.where((here != under) & (under > 0), 1.0, 0.0)
        whole_cross.append(differs)
        differs = jnp.where(inside, differs, 0.0)
        cross[d * ROWS : (d + 1) * ROWS] = differs
        value[d * ROWS : (d + 1) * ROWS] = differs * soft[d * ROWS : (d + 1) * ROWS]
    pad = jnp.zeros((XD - PART, XD), f32)
    numbers = slots[...]
    kinds = jnp.concatenate(
        whole_cross + [pad, (numbers >> 7).astype(f32), pad, (numbers & 127).astype(f32), pad], axis=0
    )
    ends[...] = along(pick_ends(), kinds.astype(bf16))

    group = 16

    def step(i, total):
        a_parts, b_parts = [], []
        base = pl.multiple_of(i * group, group)
        slot_g, value_g, cross_g = slots[pl.ds(base, group)], value[pl.ds(base, group)], cross[pl.ds(base, group)]
        for j in range(group):
            slot = slot_g[j : j + 1]
            a_parts.append(pair_hot(slot >> 7, HIGH, value_g[j : j + 1], cross_g[j : j + 1]))
            b_parts.append(one_hot(slot & 127, LANES))
        return total + along(jnp.concatenate(a_parts, axis=1), jnp.concatenate(b_parts, axis=1))

    sums[...] = lax.fori_loop(0, PART // group, step, jnp.zeros((2 * HIGH, LANES), f32))


def send_kernel(taps, logits, left, right, ids_ends, ends, sums, bucket, affinity, outgoing):
    row = iota((8, DEPTH), 0)
    left_row = jnp.where(row == 0, left[:, :DEPTH], 0.0).astype(bf16)
    right_row = jnp.where(row == 0, right[:, :DEPTH], 0.0).astype(bf16)
    first = along(taps[:PART], left_row)[:, 0:1]
    last = along(taps[2 * PART :], right_row)[:, 0:1]
    lane = iota((PART, XD), 1)
    soft = sigmoid(logits[...] + jnp.where(lane == 0, first, jnp.where(lane == XD - 1, last, 0.0)))
    affinity[...] = soft
    soft = along(pick_ends(), soft)
    soft = jnp.concatenate([soft, jnp.zeros((8, XD - PART), f32)], axis=1)

    beside = left[:, DEPTH : DEPTH + ROWS] * 128.0 + left[:, DEPTH + ROWS :]
    here = ids_ends[:, DEPTH : DEPTH + ROWS] * 128.0 + ids_ends[:, DEPTH + ROWS :]
    differs = jnp.where((beside != here) & (beside > 0.0), 1.0, 0.0)
    differs = jnp.concatenate([jnp.zeros((1, 2 * ROWS), f32), differs, jnp.zeros((1, XD - PART), f32)], axis=1)
    total = sums[...]
    a_parts, b_parts = [], []
    for end in range(2):
        cross = ends[end : end + 1, :XD]
        if end == 0:
            cross = cross + differs
        high = ends[end : end + 1, XD : 2 * XD].astype(i32)
        low = ends[end : end + 1, 2 * XD :].astype(i32)
        a_parts.append(pair_hot(high, HIGH, soft[end : end + 1] * cross, cross))
        b_parts.append(one_hot(low, LANES))
    total += along(jnp.concatenate(a_parts, axis=1), jnp.concatenate(b_parts, axis=1))
    total = total.astype(bf16).astype(f32)

    sent = jnp.zeros((LANES, LANES), f32)
    for h0 in range(0, HIGH, 16):
        a_parts, b_parts = [], []
        for h in range(h0, h0 + 16):
            place = bucket[h : h + 1]
            a_parts.append(one_hot(place >> 6, LANES))
            b_parts.append(pair_hot(place & 63, BUCKET, total[h : h + 1], total[HIGH + h : HIGH + h + 1]))
        sent += along(jnp.concatenate(a_parts, axis=1), jnp.concatenate(b_parts, axis=1))
    outgoing[...] = sent


def edges_kernel(arrived, rows, mean):
    n = arrived.shape[0]
    same = jnp.where(iota((n, n), 0) == iota((n, n), 1), 1.0, 0.0).astype(bf16)
    got = lax.dot_general(arrived[...].astype(bf16), same, (((0,), (0,)), ((), ())), preferred_element_type=f32)
    total = jnp.zeros((2 * HIGH, LANES), f32)
    for q0 in range(0, BUCKET, 16):
        a_parts, b_parts = [], []
        for q in range(q0, q0 + 16):
            target = rows[q : q + 1]
            a_parts.append(pair_hot(target >> 7, HIGH, got[q : q + 1], got[BUCKET + q : BUCKET + q + 1]))
            b_parts.append(one_hot(target & 127, LANES))
        total += along(jnp.concatenate(a_parts, axis=1), jnp.concatenate(b_parts, axis=1))
    mean[...] = total[:HIGH] / jnp.maximum(total[HIGH:], 1.0)


def passed(block, axis, distance):
    size = lax.axis_size(axis)
    return lax.ppermute(block, axis, [(i, i + distance) for i in range(size) if 0 <= i + distance < size])


def local(features, conv_weight, conv_bias, fragments, pair_slot, slot_bucket, arrival_row):
    devices = lax.axis_size("gz") * lax.axis_size("yx")
    cells = features.reshape(CELLS, XD)
    ids = fragments.reshape(ROWS, XD)
    slots = pair_slot.reshape(PART, XD)
    bucket = slot_bucket.reshape(HIGH, LANES)
    weights = conv_weight.transpose(0, 2, 3, 4, 1).reshape(27, 3, C_IN)
    scalar = pl.BlockSpec(memory_space=pltpu.SMEM)
    up, down = pl.pallas_call(
        rows_kernel,
        out_shape=(near((CZ, XD), bf16), near((CZ + 2 * Z, XD), bf16)),
        in_specs=whole(2),
        out_specs=tuple(whole(2)),
    )(cells, ids)
    top = held(passed(down, "yx", 1))
    bottom = held(passed(up, "yx", -1))
    taps, logits = pl.pallas_call(
        taps_kernel,
        out_shape=(near((TAP_ROWS, DEPTH), bf16), near((PART, XD), f32)),
        in_specs=whole(2) + [scalar],
        out_specs=tuple(whole(2)),
        scratch_shapes=[pltpu.VMEM((27 * 8, LANES), f32)],
    )(cells, weights, conv_bias)
    to_left, to_right = pl.pallas_call(
        columns_kernel,
        out_shape=(near((1, WIDE), f32), near((1, WIDE), f32)),
        in_specs=whole(5),
        out_specs=tuple(whole(2)),
        scratch_shapes=[pltpu.VMEM((WIDE, XD), bf16)],
    )(cells, top, bottom, ids, held(logits))
    left = held(passed(to_right, "gz", 1))
    right = held(passed(to_left, "gz", -1))
    taps = held(taps)
    logits, sums, ends = pl.pallas_call(
        inner_kernel,
        out_shape=(near((PART, XD), f32), near((2 * HIGH, LANES), f32), near((8, 3 * XD), f32)),
        in_specs=whole(6),
        out_specs=tuple(whole(3)),
        scratch_shapes=[pltpu.VMEM((LANES, XD), bf16), pltpu.VMEM((PART, XD), f32), pltpu.VMEM((PART, XD), f32)],
    )(taps, held(logits), top, bottom, ids, slots)
    affinity, outgoing = pl.pallas_call(
        send_kernel,
        out_shape=(jax.ShapeDtypeStruct((PART, XD), bf16), near((devices, 2 * BUCKET), f32)),
        in_specs=whole(8),
        out_specs=tuple(whole(2)),
    )(taps, held(logits), left, right, held(to_left), held(ends), held(sums), bucket)
    arrived = lax.all_to_all(outgoing, ("gz", "yx"), split_axis=0, concat_axis=0, tiled=True)
    mean = pl.pallas_call(
        edges_kernel,
        out_shape=jax.ShapeDtypeStruct((HIGH, LANES), f32),
        in_specs=whole(2),
        out_specs=whole(1)[0],
    )(held(arrived), arrival_row[0].T)
    return affinity.reshape(C_OUT, Z, YD, XD), mean.reshape(E_OWN)


def solution(mesh):
    return jax.shard_map(
        local,
        mesh=mesh,
        in_specs=(
            P(None, None, "yx", "gz"),
            P(),
            P(),
            P(None, "yx", "gz"),
            P(None, None, "yx", "gz"),
            P(("gz", "yx"), None),
            P(("gz", "yx"), None, None),
        ),
        out_specs=(P(None, None, "yx", "gz"), P(("gz", "yx"))),
        check_vma=False,
    )
```

```python
import functools

import jax
import jax.numpy as jnp
from jax import lax
from jax.experimental import pallas as pl
from jax.experimental.pallas import tpu as pltpu
from jax.sharding import PartitionSpec as P

C_IN, C_OUT, Z, YD, XD = 12, 3, 4, 16, 256
BUCKET, E_OWN, P_LOC = 64, 4096, 4096
CZ = C_IN * Z
CELLS = CZ * YD
DEPTH = CELLS + 2 * CZ + 32
WIDE = DEPTH + 2 * Z * YD
ROWS = Z * YD
LANES = 128
HIGH = P_LOC // LANES

TAP_ROWS = 9 * ROWS
PART = C_OUT * ROWS
EARLY = 7

f32, bf16, i32 = jnp.float32, jnp.bfloat16, jnp.int32


def iota(shape, dim):
    return lax.broadcasted_iota(i32, shape, dim)


def along(a, b):
    return lax.dot_general(a, b, (((1,), (1,)), ((), ())), preferred_element_type=f32)


def whole(count):
    return [pl.BlockSpec(memory_space=pltpu.VMEM)] * count


def near(shape, dtype):
    return pltpu.VMEM(shape, dtype)


def held(x):
    return pltpu.with_memory_space_constraint(x, pltpu.VMEM)


def even(axis):
    return lax.rem(lax.axis_index(axis), 2) == 0


def rows_kernel(*refs):
    sources, (one, two), held_refs, sems = refs[:6], refs[6:8], refs[8:14], refs[14]
    copies = [pltpu.make_async_copy(a, b, sems.at[i]) for i, (a, b) in enumerate(zip(sources, held_refs))]
    for copy in copies:
        copy.start()
    cells, ids = held_refs[:2]
    row = iota((2 * CZ, CELLS), 0)
    inner = jnp.where(even("yx"), YD - 1, 0)
    wanted = jnp.where(row < CZ, row * YD + inner, (row - CZ) * YD + (YD - 1 - inner))
    pick = jnp.where(iota((2 * CZ, CELLS), 1) == wanted, 1.0, 0.0).astype(bf16)
    copies[0].wait()
    picked = jnp.dot(pick, cells[...], preferred_element_type=f32).astype(bf16)
    copies[1].wait()
    last = jnp.concatenate([ids[(z + 1) * YD - 1 : (z + 1) * YD] for z in range(Z)], axis=0)
    pair = jnp.concatenate([last >> 7, last & 127], axis=0).astype(f32).astype(bf16)
    one[:CZ] = picked[:CZ]
    two[:CZ] = picked[CZ:]
    one[CZ:] = pair
    two[CZ:] = pair
    for copy in copies[2:]:
        copy.wait()


def placed(inner, outer, axis):
    first = even(axis)
    return jnp.where(first, outer, inner), jnp.where(first, inner, outer)


def pick_ends():
    row, lane = iota((8, XD), 0), iota((8, XD), 1)
    return jnp.where((row < 2) & (lane == row * (XD - 1)), 1.0, 0.0).astype(bf16)


def columns_kernel(cells, one, two, ids, after, inner, outer, own, wide):
    top, bottom = placed(one[:CZ], two[:CZ], "yx")
    wide[:CELLS] = cells[...]
    wide[CELLS : CELLS + CZ] = top
    wide[CELLS + CZ : CELLS + 2 * CZ] = bottom
    wide[CELLS + 2 * CZ : DEPTH] = jnp.zeros((DEPTH - CELLS - 2 * CZ, XD), bf16)
    wide[DEPTH : DEPTH + ROWS] = (ids[...] >> 7).astype(f32).astype(bf16)
    wide[DEPTH + ROWS :] = (ids[...] & 127).astype(f32).astype(bf16)
    picked = along(pick_ends(), wide[...])
    first = even("gz")
    inner[...] = jnp.where(first, picked[1:2], picked[0:1])
    outer[...] = jnp.where(first, picked[0:1], picked[1:2])
    own[...] = picked[0:1]


def taps_kernel(cells, weights, bias, ids, slots, taps, logits, sums, flat, value, cross):
    flat[...] = jnp.zeros(flat.shape, f32)
    for i in range(27):
        flat[8 * i : 8 * i + 3, :C_IN] = weights[i].astype(f32)
    k = iota((LANES, DEPTH), 1)
    channel = jnp.where(k < CELLS, k // (Z * YD), ((k - CELLS) % CZ) // Z)
    channel = jnp.where(k < CELLS + 2 * CZ, channel, LANES)
    spread = jnp.where(iota((LANES, DEPTH), 0) == channel, 1.0, 0.0).astype(bf16)
    lines = jnp.dot(flat[...].astype(bf16), spread, preferred_element_type=f32)
    for t in range(DEPTH // LANES):
        y, k = iota((YD, LANES), 0), iota((YD, LANES), 1) + t * LANES
        inner = k < CELLS
        z_in = jnp.where(inner, (k // YD) % Z, (k - CELLS) % Z)
        y_in = jnp.where(inner, k % YD, jnp.where(k < CELLS + CZ, -1, YD))
        y_in = jnp.where(k < CELLS + 2 * CZ, y_in, 3 * YD)
        dy = y_in - y + 1
        for e in range(3):
            for o in range(C_OUT):
                bands = []
                for a in range(3):
                    band = jnp.zeros((YD, LANES), f32)
                    for b in range(3):
                        r = (o * 9 + a * 3 + b) * 8 + e
                        band = jnp.where(dy == b, lines[r : r + 1, t * LANES : (t + 1) * LANES], band)
                    bands.append(band)
                for z in range(Z):
                    tap = jnp.zeros((YD, LANES), f32)
                    for a in range(3):
                        if 0 <= z + a - 1 < Z:
                            tap = jnp.where(z_in == z + a - 1, bands[a], tap)
                    row = ((e * C_OUT + o) * Z + z) * YD
                    taps[row : row + YD, t * LANES : (t + 1) * LANES] = tap.astype(bf16)
    product = jnp.dot(taps[:, :CELLS], cells[...], preferred_element_type=f32)
    channel = iota((PART, XD), 0) // ROWS
    bias = jnp.where(channel == 0, bias[0], jnp.where(channel == 1, bias[1], bias[2]))
    total = shifted(product) + bias
    logits[...] = total
    rows = EARLY * YD
    fill_pairs(total[:rows], crossings(ids[...], None)[:rows], value, cross)
    sums[...] = pair_sums(1, EARLY, range(1, YD - 1), slots, value, cross)


def shifted(product):
    lane = iota((PART, XD), 1)
    total = product[PART : 2 * PART]
    total += jnp.where(lane == 0, 0.0, pltpu.roll(product[:PART], 1, 1))
    return total + jnp.where(lane == XD - 1, 0.0, pltpu.roll(product[2 * PART :], XD - 1, 1))


def sigmoid(x):
    return (1.0 / (1.0 + jnp.exp(-x))).astype(bf16)


def one_hot(line, count, value=None):
    hit = iota((count, line.shape[1]), 0) == line
    return jnp.where(hit, 1.0 if value is None else value, 0.0).astype(bf16)


def pair_hot(line, count, first, second):
    return jnp.concatenate([one_hot(line, count, first), one_hot(line, count, second)], axis=0)


def crossings(here, above):
    m, n = iota((ROWS, XD), 0), iota((ROWS, XD), 1)
    under_z = jnp.concatenate([here[:YD], here[:-YD]], axis=0)
    under_y = pltpu.roll(here, 1, 0)
    if above is not None:
        above = jnp.concatenate([jnp.broadcast_to(above[z : z + 1], (YD, XD)) for z in range(Z)], axis=0)
        under_y = jnp.where(m % YD == 0, above, under_y)
    under_x = jnp.where(n == 0, here, pltpu.roll(here, 1, 1))
    unders = (under_z, under_y, under_x)
    return jnp.concatenate([jnp.where((here != under) & (under > 0), 1.0, 0.0) for under in unders], axis=0)


def fill_pairs(logits, crossed, value, cross):
    n = iota(logits.shape, 1)
    crossed = jnp.where((n > 0) & (n < XD - 1), crossed, 0.0)
    cross[...] = crossed
    value[...] = crossed * sigmoid(logits).astype(f32)


def chunk_sums(chunks):
    a_parts = [pair_hot(slot >> 7, HIGH, value, cross) for slot, value, cross in chunks]
    b_parts = [one_hot(slot & 127, LANES) for slot, _, _ in chunks]
    return along(jnp.concatenate(a_parts, axis=1), jnp.concatenate(b_parts, axis=1))


def pair_sums(first, count, rows, slots, value, cross):
    def step(i, total):
        base = pl.multiple_of(i * YD, YD)
        tiles = slots[pl.ds(base, YD)], value[pl.ds(base, YD)], cross[pl.ds(base, YD)]
        return total + chunk_sums([[tile[j : j + 1] for tile in tiles] for j in rows])

    return lax.fori_loop(first, count, step, jnp.zeros((2 * HIGH, LANES), f32))


def inner_kernel(taps, logits, early, one, two, ids, slots, full, sums, ends, halo, value, cross):
    top, bottom = placed(one[...].astype(f32), two[...].astype(f32), "yx")
    halo[:CZ] = top[:CZ].astype(bf16)
    halo[CZ : 2 * CZ] = bottom[:CZ].astype(bf16)
    halo[2 * CZ :] = jnp.zeros((LANES - 2 * CZ, XD), bf16)
    total = logits[...] + shifted(jnp.dot(taps[:, CELLS:], halo[...], preferred_element_type=f32))
    full[...] = total
    above = top[CZ:]
    above = (above[:Z] * 128.0 + above[Z:]).astype(i32)
    crossed = crossings(ids[...], above)
    fill_pairs(total, crossed, value, cross)
    pad = jnp.zeros((XD - PART, XD), f32)
    numbers = slots[...]
    kinds = [crossed, pad, (numbers >> 7).astype(f32), pad, (numbers & 127).astype(f32), pad]
    ends[...] = along(pick_ends(), jnp.concatenate(kinds, axis=0).astype(bf16))
    outer = [i * YD + y for i in range(1, EARLY) for y in (0, YD - 1)]
    sums[...] = (
        early[...]
        + chunk_sums([[ref[j : j + 1] for ref in (slots, value, cross)] for j in outer])
        + pair_sums(EARLY, C_OUT * Z, range(YD), slots, value, cross)
    )


def send_kernel(taps, logits, inner, outer, own, ends, sums, bucket, first, last, outgoing):
    left, right = placed(inner[...], outer[...], "gz")
    row = iota((8, DEPTH), 0)
    left_row = jnp.where(row == 0, left[:, :DEPTH], 0.0).astype(bf16)
    right_row = jnp.where(row == 0, right[:, :DEPTH], 0.0).astype(bf16)
    first[...] = along(taps[:PART], left_row)
    last[...] = along(taps[2 * PART :], right_row)
    lane = iota((PART, LANES), 1)
    low = logits[:, :LANES] + first[:, 0:1]
    high = logits[:, XD - LANES :] + last[:, 0:1]
    soft = sigmoid(jnp.where(lane < LANES // 2, low, high))
    row, lane = iota((8, LANES), 0), iota((8, LANES), 1)
    pick = jnp.where((row < 2) & (lane == row * (LANES - 1)), 1.0, 0.0).astype(bf16)
    soft = jnp.concatenate([along(pick, soft), jnp.zeros((8, XD - PART), f32)], axis=1)

    beside = left[:, DEPTH : DEPTH + ROWS] * 128.0 + left[:, DEPTH + ROWS :]
    here = own[:, DEPTH : DEPTH + ROWS] * 128.0 + own[:, DEPTH + ROWS :]
    differs = jnp.where((beside != here) & (beside > 0.0), 1.0, 0.0)
    differs = jnp.concatenate([jnp.zeros((1, 2 * ROWS), f32), differs, jnp.zeros((1, XD - PART), f32)], axis=1)
    chunks = []
    for end in range(2):
        crossed = ends[end : end + 1, :XD]
        if end == 0:
            crossed = crossed + differs
        slot = ends[end : end + 1, XD : 2 * XD] * 128.0 + ends[end : end + 1, 2 * XD :]
        chunks.append((slot.astype(i32), soft[end : end + 1] * crossed, crossed))
    total = sums[...] + chunk_sums(chunks)
    total = total.astype(bf16).astype(f32)

    sent = jnp.zeros((LANES, LANES), f32)
    for h0 in range(0, HIGH, 16):
        a_parts, b_parts = [], []
        for h in range(h0, h0 + 16):
            place = bucket[h : h + 1]
            a_parts.append(one_hot(place >> 6, LANES))
            b_parts.append(pair_hot(place & 63, BUCKET, total[h : h + 1], total[HIGH + h : HIGH + h + 1]))
        sent += along(jnp.concatenate(a_parts, axis=1), jnp.concatenate(b_parts, axis=1))
    outgoing[...] = sent


def affinity_kernel(logits, first, last, affinity):
    lane = iota((PART, XD), 1)
    outer = jnp.where(lane == 0, first[:, 0:1], jnp.where(lane == XD - 1, last[:, 0:1], 0.0))
    affinity[...] = sigmoid(logits[...] + outer)


def edges_kernel(arrived, rows, mean):
    n = arrived.shape[0]
    same = jnp.where(iota((n, n), 0) == iota((n, n), 1), 1.0, 0.0).astype(bf16)
    got = lax.dot_general(arrived[...].astype(bf16), same, (((0,), (0,)), ((), ())), preferred_element_type=f32)
    total = jnp.zeros((2 * HIGH, LANES), f32)
    for q0 in range(0, BUCKET, 16):
        a_parts, b_parts = [], []
        for q in range(q0, q0 + 16):
            target = rows[q : q + 1]
            a_parts.append(pair_hot(target >> 7, HIGH, got[q : q + 1], got[BUCKET + q : BUCKET + q + 1]))
            b_parts.append(one_hot(target & 127, LANES))
        total += along(jnp.concatenate(a_parts, axis=1), jnp.concatenate(b_parts, axis=1))
    mean[...] = total[:HIGH] / jnp.maximum(total[HIGH:], 1.0)


def swapped(block, axis, first):
    pairs = [(i, i + 1) for i in range(first, lax.axis_size(axis) - 1, 2)]
    return held(lax.ppermute(block, axis, pairs + [(j, i) for i, j in pairs]))


def local(features, conv_weight, conv_bias, fragments, pair_slot, slot_bucket, arrival_row):
    devices = lax.axis_size("gz") * lax.axis_size("yx")
    inputs = (
        features.reshape(CELLS, XD),
        fragments.reshape(ROWS, XD),
        pair_slot.reshape(PART, XD),
        conv_weight.transpose(0, 2, 3, 4, 1).reshape(27, 3, C_IN),
        slot_bucket.reshape(HIGH, LANES),
        arrival_row[0].T,
    )
    scalar = pl.BlockSpec(memory_space=pltpu.SMEM)
    pairs = [pltpu.VMEM((PART, XD), f32)] * 2
    sums_shape = near((2 * HIGH, LANES), f32)
    lines = near((CZ + 2 * Z, XD), bf16)
    one, two, *inputs = pl.pallas_call(
        rows_kernel,
        out_shape=(lines, lines, *(near(x.shape, x.dtype) for x in inputs)),
        in_specs=[pl.BlockSpec(memory_space=pl.ANY)] * 6,
        out_specs=tuple(whole(8)),
        scratch_shapes=[pltpu.SemaphoreType.DMA((6,))],
    )(*inputs)
    cells, ids, slots, weights, bucket, targets = map(held, inputs)
    two = swapped(two, "yx", 1)
    one = swapped(one, "yx", 0)
    taps, logits, early = pl.pallas_call(
        taps_kernel,
        out_shape=(near((TAP_ROWS, DEPTH), bf16), near((PART, XD), f32), sums_shape),
        in_specs=whole(2) + [scalar] + whole(2),
        out_specs=tuple(whole(3)),
        scratch_shapes=[pltpu.VMEM((27 * 8, LANES), f32)] + [pltpu.VMEM((EARLY * YD, XD), f32)] * 2,
    )(cells, weights, conv_bias, ids, slots)
    taps, logits, early = held(taps), held(logits), held(early)
    inner, outer, own = pl.pallas_call(
        columns_kernel,
        out_shape=(near((1, WIDE), f32),) * 3,
        in_specs=whole(5),
        out_specs=tuple(whole(3)),
        scratch_shapes=[pltpu.VMEM((WIDE, XD), bf16)],
    )(cells, one, two, ids, early)
    outer = swapped(outer, "gz", 1)
    inner = swapped(inner, "gz", 0)
    logits, sums, ends = pl.pallas_call(
        inner_kernel,
        out_shape=(near((PART, XD), f32), sums_shape, near((8, 3 * XD), f32)),
        in_specs=whole(7),
        out_specs=tuple(whole(3)),
        scratch_shapes=[pltpu.VMEM((LANES, XD), bf16)] + pairs,
    )(taps, logits, early, one, two, ids, slots)
    logits = held(logits)
    first, last, outgoing = pl.pallas_call(
        send_kernel,
        out_shape=(near((PART, 8), f32), near((PART, 8), f32), near((devices, 2 * BUCKET), f32)),
        in_specs=whole(8),
        out_specs=tuple(whole(3)),
    )(taps, logits, inner, outer, held(own), held(ends), held(sums), bucket)
    arrived = lax.all_to_all(outgoing, ("gz", "yx"), split_axis=0, concat_axis=0, tiled=True)
    affinity = pl.pallas_call(
        affinity_kernel,
        out_shape=jax.ShapeDtypeStruct((PART, XD), bf16),
        in_specs=whole(3),
        out_specs=whole(1)[0],
    )(logits, held(first), held(last))
    mean = pl.pallas_call(
        edges_kernel,
        out_shape=jax.ShapeDtypeStruct((HIGH, LANES), f32),
        in_specs=whole(2),
        out_specs=whole(1)[0],
    )(held(arrived), targets)
    return affinity.reshape(C_OUT, Z, YD, XD), mean.reshape(E_OWN)


def solution(mesh):
    return jax.shard_map(
        local,
        mesh=mesh,
        in_specs=(
            P(None, None, "yx", "gz"),
            P(),
            P(),
            P(None, "yx", "gz"),
            P(None, None, "yx", "gz"),
            P(("gz", "yx"), None),
            P(("gz", "yx"), None, None),
        ),
        out_specs=(P(None, None, "yx", "gz"), P(("gz", "yx"))),
        check_vma=False,
    )
```

```python
import functools

import jax
import jax.numpy as jnp
from jax import lax
from jax.experimental import pallas as pl
from jax.experimental.pallas import tpu as pltpu
from jax.sharding import PartitionSpec as P

C_IN, C_OUT, Z, YD, XD = 12, 3, 4, 16, 256
BUCKET, E_OWN, P_LOC = 64, 4096, 4096
CZ = C_IN * Z
CELLS = CZ * YD
DEPTH = CELLS + 2 * CZ + 32
WIDE = DEPTH + 2 * Z * YD
ROWS = Z * YD
LANES = 128
HIGH = P_LOC // LANES

TAP_ROWS = 9 * ROWS
PART = C_OUT * ROWS
EARLY = 7
BATCH = 48
LOW, HALF, STEP = 96, 48, 12

f32, bf16, i32 = jnp.float32, jnp.bfloat16, jnp.int32


def iota(shape, dim):
    return lax.broadcasted_iota(i32, shape, dim)


def along(a, b):
    return lax.dot_general(a, b, (((1,), (1,)), ((), ())), preferred_element_type=f32)


def whole(count):
    return [pl.BlockSpec(memory_space=pltpu.VMEM)] * count


def near(shape, dtype):
    return pltpu.VMEM(shape, dtype)


def held(x):
    return pltpu.with_memory_space_constraint(x, pltpu.VMEM)


def even(axis):
    return lax.rem(lax.axis_index(axis), 2) == 0


def rows_kernel(*refs):
    count = len(refs) // 2 - 1
    sources, (one, two), held_refs, sems = refs[:count], refs[count : count + 2], refs[count + 2 : -1], refs[-1]
    copies = [pltpu.make_async_copy(a, b, sems.at[i]) for i, (a, b) in enumerate(zip(sources, held_refs))]
    for copy in copies:
        copy.start()
    cells, ids = held_refs[:2]
    row = iota((2 * CZ, CELLS), 0)
    inner = jnp.where(even("yx"), YD - 1, 0)
    wanted = jnp.where(row < CZ, row * YD + inner, (row - CZ) * YD + (YD - 1 - inner))
    pick = jnp.where(iota((2 * CZ, CELLS), 1) == wanted, 1.0, 0.0).astype(bf16)
    copies[0].wait()
    picked = jnp.dot(pick, cells[...], preferred_element_type=f32).astype(bf16)
    copies[1].wait()
    last = jnp.concatenate([ids[(z + 1) * YD - 1 : (z + 1) * YD] for z in range(Z)], axis=0)
    pair = jnp.concatenate([last >> 7, last & 127], axis=0).astype(f32).astype(bf16)
    one[:CZ] = picked[:CZ]
    two[:CZ] = picked[CZ:]
    one[CZ:] = pair
    two[CZ:] = pair
    for copy in copies[2:]:
        copy.wait()


def placed(inner, outer, axis):
    first = even(axis)
    return jnp.where(first, outer, inner), jnp.where(first, inner, outer)


def pick_ends():
    row, lane = iota((8, XD), 0), iota((8, XD), 1)
    return jnp.where((row < 2) & (lane == row * (XD - 1)), 1.0, 0.0).astype(bf16)


def columns_kernel(two, one, cells, ids, after, inner, outer, own, wide):
    top, bottom = placed(one[:CZ], two[:CZ], "yx")
    wide[:CELLS] = cells[...]
    wide[CELLS : CELLS + CZ] = top
    wide[CELLS + CZ : CELLS + 2 * CZ] = bottom
    wide[CELLS + 2 * CZ : DEPTH] = jnp.zeros((DEPTH - CELLS - 2 * CZ, XD), bf16)
    wide[DEPTH : DEPTH + ROWS] = (ids[...] >> 7).astype(f32).astype(bf16)
    wide[DEPTH + ROWS :] = (ids[...] & 127).astype(f32).astype(bf16)
    picked = along(pick_ends(), wide[...])
    first = even("gz")
    inner[...] = jnp.where(first, picked[1:2], picked[0:1])
    outer[...] = jnp.where(first, picked[0:1], picked[1:2])
    own[...] = picked[0:1]


def taps_kernel(cells, weights, bias, ids, slots, taps, logits, sums, flat, value, cross):
    flat[...] = jnp.zeros(flat.shape, f32)
    for i in range(27):
        flat[8 * i : 8 * i + 3, :C_IN] = weights[i].astype(f32)
    k = iota((LANES, DEPTH), 1)
    channel = jnp.where(k < CELLS, k // (Z * YD), ((k - CELLS) % CZ) // Z)
    channel = jnp.where(k < CELLS + 2 * CZ, channel, LANES)
    spread = jnp.where(iota((LANES, DEPTH), 0) == channel, 1.0, 0.0).astype(bf16)
    lines = jnp.dot(flat[...].astype(bf16), spread, preferred_element_type=f32).astype(bf16)
    for t in range(DEPTH // LANES):
        y, k = iota((YD, LANES), 0), iota((YD, LANES), 1) + t * LANES
        inner = k < CELLS
        z_in = small(jnp.where(inner, (k // YD) % Z, (k - CELLS) % Z))
        y_in = jnp.where(inner, k % YD, jnp.where(k < CELLS + CZ, -1, YD))
        y_in = jnp.where(k < CELLS + 2 * CZ, y_in, 3 * YD)
        dy = small(y_in - y + 1)
        for e in range(3):
            for o in range(C_OUT):
                bands = []
                for a in range(3):
                    band = jnp.zeros((YD, LANES), bf16)
                    for b in range(3):
                        r = (o * 9 + a * 3 + b) * 8 + e
                        band = jnp.where(dy == float(b), lines[r : r + 1, t * LANES : (t + 1) * LANES], band)
                    bands.append(band)
                for z in range(Z):
                    tap = jnp.zeros((YD, LANES), bf16)
                    for a in range(3):
                        if 0 <= z + a - 1 < Z:
                            tap = jnp.where(z_in == float(z + a - 1), bands[a], tap)
                    row = ((e * C_OUT + o) * Z + z) * YD
                    taps[row : row + YD, t * LANES : (t + 1) * LANES] = tap
    product = jnp.dot(taps[:, :CELLS], cells[...], preferred_element_type=f32)
    offset = jnp.concatenate([jnp.broadcast_to(bias[:, o : o + 1], (ROWS, 1)) for o in range(C_OUT)], axis=0)
    total = shifted(product) + offset
    logits[...] = total
    rows = EARLY * YD
    fill_pairs(total[:rows], crossings(ids[...], None)[:rows], value, cross)
    sums[...] = batched([line for i in range(1, EARLY) for line in lines_of(i, range(1, YD - 1), slots, value, cross)])


def shifted(product):
    lane = iota((PART, XD), 1)
    total = product[PART : 2 * PART]
    total += jnp.where(lane == 0, 0.0, pltpu.roll(product[:PART], 1, 1))
    return total + jnp.where(lane == XD - 1, 0.0, pltpu.roll(product[2 * PART :], XD - 1, 1))


def sigmoid(x):
    return (1.0 / (1.0 + jnp.exp(-x))).astype(bf16)


def one_hot(line, count, value=None):
    rows = iota((count, line.shape[1]), 0).astype(f32).astype(bf16)
    return jnp.where(rows == line, jnp.ones((), bf16) if value is None else value, jnp.zeros((), bf16))


def pair_hot(line, count, first, second):
    return jnp.concatenate([one_hot(line, count, first), one_hot(line, count, second)], axis=0)


def small(x):
    return x.astype(f32).astype(bf16)


def split(number):
    q = ((number >> 5) * 171) >> 9
    return small((q & 3) * STEP + (q >> 2)), small(number - q * LOW)


def chunk_sums(chunks):
    a_parts = [pair_hot(row, HALF, value, cross) for row, _, value, cross in chunks]
    b_parts = [one_hot(column, LOW) for _, column, _, _ in chunks]
    return along(jnp.concatenate(a_parts, axis=1), jnp.concatenate(b_parts, axis=1))


def relaid(total):
    a, b, c, d = (total[j * STEP : (j + 1) * STEP] for j in range(4))
    return (
        jnp.concatenate([a, b[:, :32]], axis=1),
        jnp.concatenate([b[:, 32:], c[:, :64]], axis=1),
        jnp.concatenate([c[:, 64:], d], axis=1),
    )


def crossings(here, above):
    m, n = iota((ROWS, XD), 0), iota((ROWS, XD), 1)
    under_z = jnp.concatenate([here[:YD], here[:-YD]], axis=0)
    under_y = pltpu.roll(here, 1, 0)
    if above is not None:
        above = jnp.concatenate([jnp.broadcast_to(above[z : z + 1], (YD, XD)) for z in range(Z)], axis=0)
        under_y = jnp.where(m % YD == 0, above, under_y)
    under_x = jnp.where(n == 0, here, pltpu.roll(here, 1, 1))
    unders = (under_z, under_y, under_x)
    return jnp.concatenate([jnp.where((here != under) & (under > 0), 1.0, 0.0) for under in unders], axis=0)


def fill_pairs(logits, crossed, value, cross):
    n = iota(logits.shape, 1)
    crossed = jnp.where((n > 0) & (n < XD - 1), crossed, 0.0)
    cross[...] = crossed
    value[...] = crossed * sigmoid(logits).astype(f32)


def lines_of(i, rows, slots, value, cross):
    at = slice(i * YD, (i + 1) * YD)
    tiles = (*split(slots[at]), value[at].astype(bf16), cross[at].astype(bf16))
    return [[tile[j : j + 1] for tile in tiles] for j in rows]


def batched(chunks, size=BATCH):
    return sum(chunk_sums(chunks[i : i + size]) for i in range(0, len(chunks), size))


def inner_kernel(two, one, taps, logits, early, ids, slots, full, sums, ends, halo, value, cross):
    top, bottom = placed(one[...].astype(f32), two[...].astype(f32), "yx")
    halo[:CZ] = top[:CZ].astype(bf16)
    halo[CZ : 2 * CZ] = bottom[:CZ].astype(bf16)
    halo[2 * CZ :] = jnp.zeros((LANES - 2 * CZ, XD), bf16)
    total = logits[...] + shifted(jnp.dot(taps[:, CELLS:], halo[...], preferred_element_type=f32))
    full[...] = total
    above = top[CZ:]
    above = (above[:Z] * 128.0 + above[Z:]).astype(i32)
    crossed = crossings(ids[...], above)
    fill_pairs(total, crossed, value, cross)
    pad = jnp.zeros((XD - PART, XD), f32)
    numbers = slots[...]
    kinds = [crossed, pad, (numbers >> 7).astype(f32), pad, (numbers & 127).astype(f32), pad]
    ends[...] = along(pick_ends(), jnp.concatenate(kinds, axis=0).astype(bf16))
    chunks = [line for i in range(1, EARLY) for line in lines_of(i, (0, YD - 1), slots, value, cross)]
    chunks += [line for i in range(EARLY, C_OUT * Z) for line in lines_of(i, range(YD), slots, value, cross)]
    sums[...] = early[...] + batched(chunks)


def send_kernel(outer, inner, taps, logits, own, ends, sums, bucket, first, last, outgoing):
    left, right = placed(inner[...], outer[...], "gz")
    row = iota((8, DEPTH), 0)
    left_row = jnp.where(row == 0, left[:, :DEPTH], 0.0).astype(bf16)
    right_row = jnp.where(row == 0, right[:, :DEPTH], 0.0).astype(bf16)
    first[...] = along(taps[:PART], left_row)
    last[...] = along(taps[2 * PART :], right_row)
    lane = iota((PART, LANES), 1)
    low = logits[:, :LANES] + first[:, 0:1]
    high = logits[:, XD - LANES :] + last[:, 0:1]
    soft = sigmoid(jnp.where(lane < LANES // 2, low, high))
    row, lane = iota((8, LANES), 0), iota((8, LANES), 1)
    pick = jnp.where((row < 2) & (lane == row * (LANES - 1)), 1.0, 0.0).astype(bf16)
    soft = jnp.concatenate([along(pick, soft), jnp.zeros((8, XD - PART), f32)], axis=1)

    beside = left[:, DEPTH : DEPTH + ROWS] * 128.0 + left[:, DEPTH + ROWS :]
    here = own[:, DEPTH : DEPTH + ROWS] * 128.0 + own[:, DEPTH + ROWS :]
    differs = jnp.where((beside != here) & (beside > 0.0), 1.0, 0.0)
    differs = jnp.concatenate([jnp.zeros((1, 2 * ROWS), f32), differs, jnp.zeros((1, XD - PART), f32)], axis=1)
    chunks = []
    for end in range(2):
        crossed = ends[end : end + 1, :XD]
        if end == 0:
            crossed = crossed + differs
        slot = ends[end : end + 1, XD : 2 * XD] * 128.0 + ends[end : end + 1, 2 * XD :]
        chunks.append((*split(slot.astype(i32)), (soft[end : end + 1] * crossed).astype(bf16), crossed.astype(bf16)))
    total = sums[...] + chunk_sums(chunks)
    kinds = [relaid(total[:HALF].astype(bf16)), relaid(total[HALF:].astype(bf16))]
    owners, places = small(bucket[...] >> 6), small(bucket[...] & 63)
    a_parts, b_parts = [], []
    for h in range(HIGH):
        k, j = divmod(h, 3)
        a_parts.append(one_hot(owners[h : h + 1], LANES))
        b_parts.append(pair_hot(places[h : h + 1], BUCKET, kinds[0][j][k : k + 1], kinds[1][j][k : k + 1]))
    sent = along(jnp.concatenate(a_parts, axis=1), jnp.concatenate(b_parts, axis=1))
    outgoing[...] = sent


def affinity_kernel(logits, first, last, affinity):
    lane = iota((PART, XD), 1)
    outer = jnp.where(lane == 0, first[:, 0:1], jnp.where(lane == XD - 1, last[:, 0:1], 0.0))
    affinity[...] = sigmoid(logits[...] + outer)


def edges_kernel(arrived, rows, mean):
    n = arrived.shape[0]
    same = jnp.where(iota((n, n), 0) == iota((n, n), 1), 1.0, 0.0).astype(bf16)
    got = lax.dot_general(arrived[...].astype(bf16), same, (((0,), (0,)), ((), ())), preferred_element_type=f32)
    got = got.astype(bf16)
    row, column = split(rows[...])
    total = chunk_sums(
        [
            (row[q : q + 1], column[q : q + 1], got[q : q + 1], got[BUCKET + q : BUCKET + q + 1])
            for q in range(BUCKET)
        ]
    )
    parts = relaid(total[:HALF] / jnp.maximum(total[HALF:], 1.0))
    for h in range(HIGH):
        k, j = divmod(h, 3)
        mean[h : h + 1] = parts[j][k : k + 1]


def swapped(block, axis, first):
    pairs = [(i, i + 1) for i in range(first, lax.axis_size(axis) - 1, 2)]
    return held(lax.ppermute(block, axis, pairs + [(j, i) for i, j in pairs]))


def local(features, conv_weight, conv_bias, fragments, pair_slot, slot_bucket, arrival_row):
    devices = lax.axis_size("gz") * lax.axis_size("yx")
    inputs = (
        features.reshape(CELLS, XD),
        fragments.reshape(ROWS, XD),
        pair_slot.reshape(PART, XD),
        conv_weight.transpose(0, 2, 3, 4, 1).reshape(27, 3, C_IN),
        slot_bucket.reshape(HIGH, LANES),
        arrival_row[0].T,
        conv_bias.reshape(1, C_OUT),
    )
    pairs = [pltpu.VMEM((PART, XD), f32)] * 2
    sums_shape = near((2 * HALF, LOW), f32)
    lines = near((CZ + 2 * Z, XD), bf16)
    one, two, *inputs = pl.pallas_call(
        rows_kernel,
        out_shape=(lines, lines, *(near(x.shape, x.dtype) for x in inputs)),
        in_specs=[pl.BlockSpec(memory_space=pl.ANY)] * len(inputs),
        out_specs=tuple(whole(2 + len(inputs))),
        scratch_shapes=[pltpu.SemaphoreType.DMA((len(inputs),))],
    )(*inputs)
    cells, ids, slots, weights, bucket, targets, bias = map(held, inputs)
    two = swapped(two, "yx", 1)
    one = swapped(one, "yx", 0)
    taps, logits, early = pl.pallas_call(
        taps_kernel,
        out_shape=(near((TAP_ROWS, DEPTH), bf16), near((PART, XD), f32), sums_shape),
        in_specs=whole(5),
        out_specs=tuple(whole(3)),
        scratch_shapes=[pltpu.VMEM((27 * 8, LANES), f32)] + [pltpu.VMEM((EARLY * YD, XD), f32)] * 2,
    )(cells, weights, bias, ids, slots)
    taps, logits, early = held(taps), held(logits), held(early)
    inner, outer, own = pl.pallas_call(
        columns_kernel,
        out_shape=(near((1, WIDE), f32),) * 3,
        in_specs=whole(5),
        out_specs=tuple(whole(3)),
        scratch_shapes=[pltpu.VMEM((WIDE, XD), bf16)],
    )(two, one, cells, ids, early)
    outer = swapped(outer, "gz", 1)
    inner = swapped(inner, "gz", 0)
    logits, sums, ends = pl.pallas_call(
        inner_kernel,
        out_shape=(near((PART, XD), f32), sums_shape, near((8, 3 * XD), f32)),
        in_specs=whole(7),
        out_specs=tuple(whole(3)),
        scratch_shapes=[pltpu.VMEM((LANES, XD), bf16)] + pairs,
    )(two, one, taps, logits, early, ids, slots)
    logits = held(logits)
    first, last, outgoing = pl.pallas_call(
        send_kernel,
        out_shape=(near((PART, 8), f32), near((PART, 8), f32), near((devices, 2 * BUCKET), f32)),
        in_specs=whole(8),
        out_specs=tuple(whole(3)),
    )(outer, inner, taps, logits, held(own), held(ends), held(sums), bucket)
    arrived = lax.all_to_all(held(outgoing), ("gz", "yx"), split_axis=0, concat_axis=0, tiled=True)
    affinity = pl.pallas_call(
        affinity_kernel,
        out_shape=jax.ShapeDtypeStruct((PART, XD), bf16),
        in_specs=whole(3),
        out_specs=whole(1)[0],
    )(logits, held(first), held(last))
    mean = pl.pallas_call(
        edges_kernel,
        out_shape=jax.ShapeDtypeStruct((HIGH, LANES), f32),
        in_specs=whole(2),
        out_specs=whole(1)[0],
    )(held(arrived), targets)
    return affinity.reshape(C_OUT, Z, YD, XD), mean.reshape(E_OWN)


def solution(mesh):
    return jax.shard_map(
        local,
        mesh=mesh,
        in_specs=(
            P(None, None, "yx", "gz"),
            P(),
            P(),
            P(None, "yx", "gz"),
            P(None, None, "yx", "gz"),
            P(("gz", "yx"), None),
            P(("gz", "yx"), None, None),
        ),
        out_specs=(P(None, None, "yx", "gz"), P(("gz", "yx"))),
        check_vma=False,
    )
```

```python
import functools

import jax
import jax.numpy as jnp
from jax import lax
from jax.experimental import pallas as pl
from jax.experimental.pallas import tpu as pltpu
from jax.sharding import PartitionSpec as P

C_IN, C_OUT, Z, YD, XD = 12, 3, 4, 16, 256
BUCKET, E_OWN, P_LOC = 64, 4096, 4096
CZ = C_IN * Z
CELLS = CZ * YD
DEPTH = CELLS + 2 * CZ + 32
WIDE = DEPTH + 2 * Z * YD
ROWS = Z * YD
LANES = 128
HIGH = P_LOC // LANES

TAP_ROWS = 9 * ROWS
PART = C_OUT * ROWS
EARLY = 9
BATCH = 48
LOW, HALF, STEP = 96, 48, 12

f32, bf16, i32 = jnp.float32, jnp.bfloat16, jnp.int32


def iota(shape, dim):
    return lax.broadcasted_iota(i32, shape, dim)


def along(a, b):
    return lax.dot_general(a, b, (((1,), (1,)), ((), ())), preferred_element_type=f32)


def whole(count):
    return [pl.BlockSpec(memory_space=pltpu.VMEM)] * count


def near(shape, dtype):
    return pltpu.VMEM(shape, dtype)


def held(x):
    return pltpu.with_memory_space_constraint(x, pltpu.VMEM)


def even(axis):
    return lax.rem(lax.axis_index(axis), 2) == 0


def rows_kernel(*refs):
    count = len(refs) // 2 - 1
    sources, (one, two), held_refs, sems = refs[:count], refs[count : count + 2], refs[count + 2 : -1], refs[-1]
    copies = [pltpu.make_async_copy(a, b, sems.at[i]) for i, (a, b) in enumerate(zip(sources, held_refs))]
    for copy in copies:
        copy.start()
    cells, ids = held_refs[:2]
    row = iota((2 * CZ, CELLS), 0)
    inner = jnp.where(even("yx"), YD - 1, 0)
    wanted = jnp.where(row < CZ, row * YD + inner, (row - CZ) * YD + (YD - 1 - inner))
    pick = jnp.where(iota((2 * CZ, CELLS), 1) == wanted, 1.0, 0.0).astype(bf16)
    copies[0].wait()
    picked = jnp.dot(pick, cells[...], preferred_element_type=f32).astype(bf16)
    copies[1].wait()
    last = jnp.concatenate([ids[(z + 1) * YD - 1 : (z + 1) * YD] for z in range(Z)], axis=0)
    pair = jnp.concatenate([last >> 7, last & 127], axis=0).astype(f32).astype(bf16)
    one[:CZ] = picked[:CZ]
    two[:CZ] = picked[CZ:]
    one[CZ:] = pair
    two[CZ:] = pair
    for copy in copies[2:]:
        copy.wait()


def placed(inner, outer, axis):
    first = even(axis)
    return jnp.where(first, outer, inner), jnp.where(first, inner, outer)


def pick_ends():
    row, lane = iota((8, XD), 0), iota((8, XD), 1)
    return jnp.where((row < 2) & (lane == row * (XD - 1)), 1.0, 0.0).astype(bf16)


def columns_kernel(two, one, cells, ids, after, inner, outer, own, wide):
    top, bottom = placed(one[:CZ], two[:CZ], "yx")
    wide[:CELLS] = cells[...]
    wide[CELLS : CELLS + CZ] = top
    wide[CELLS + CZ : CELLS + 2 * CZ] = bottom
    wide[CELLS + 2 * CZ : DEPTH] = jnp.zeros((DEPTH - CELLS - 2 * CZ, XD), bf16)
    wide[DEPTH : DEPTH + ROWS] = (ids[...] >> 7).astype(f32).astype(bf16)
    wide[DEPTH + ROWS :] = (ids[...] & 127).astype(f32).astype(bf16)
    picked = along(pick_ends(), wide[...])
    first = even("gz")
    inner[...] = jnp.where(first, picked[1:2], picked[0:1])
    outer[...] = jnp.where(first, picked[0:1], picked[1:2])
    own[...] = picked[0:1]


def taps_kernel(cells, weights, bias, ids, slots, taps, logits, sums, flat, value, cross):
    flat[...] = jnp.zeros(flat.shape, f32)
    for i in range(27):
        flat[8 * i : 8 * i + 3, :C_IN] = weights[i].astype(f32)
    k = iota((LANES, DEPTH), 1)
    channel = jnp.where(k < CELLS, k // (Z * YD), ((k - CELLS) % CZ) // Z)
    channel = jnp.where(k < CELLS + 2 * CZ, channel, LANES)
    spread = jnp.where(iota((LANES, DEPTH), 0) == channel, 1.0, 0.0).astype(bf16)
    lines = jnp.dot(flat[...].astype(bf16), spread, preferred_element_type=f32).astype(bf16)
    for t in range(DEPTH // LANES):
        y, k = iota((YD, LANES), 0), iota((YD, LANES), 1) + t * LANES
        inner = k < CELLS
        z_in = small(jnp.where(inner, (k // YD) % Z, (k - CELLS) % Z))
        y_in = jnp.where(inner, k % YD, jnp.where(k < CELLS + CZ, -1, YD))
        y_in = jnp.where(k < CELLS + 2 * CZ, y_in, 3 * YD)
        dy = small(y_in - y + 1)
        for e in range(3):
            for o in range(C_OUT):
                bands = []
                for a in range(3):
                    band = jnp.zeros((YD, LANES), bf16)
                    for b in range(3):
                        r = (o * 9 + a * 3 + b) * 8 + e
                        band = jnp.where(dy == float(b), lines[r : r + 1, t * LANES : (t + 1) * LANES], band)
                    bands.append(band)
                for z in range(Z):
                    tap = jnp.zeros((YD, LANES), bf16)
                    for a in range(3):
                        if 0 <= z + a - 1 < Z:
                            tap = jnp.where(z_in == float(z + a - 1), bands[a], tap)
                    row = ((e * C_OUT + o) * Z + z) * YD
                    taps[row : row + YD, t * LANES : (t + 1) * LANES] = tap
    product = jnp.dot(taps[:, :CELLS], cells[...], preferred_element_type=f32)
    offset = jnp.concatenate([jnp.broadcast_to(bias[:, o : o + 1], (ROWS, 1)) for o in range(C_OUT)], axis=0)
    total = shifted(product) + offset
    logits[...] = total
    rows = EARLY * YD
    fill_pairs(total[:rows], crossings(ids[...], None)[:rows], value, cross)
    sums[...] = batched([line for i in range(1, EARLY) for line in lines_of(i, range(1, YD - 1), slots, value, cross)])


def shifted(product):
    lane = iota((PART, XD), 1)
    total = product[PART : 2 * PART]
    total += jnp.where(lane == 0, 0.0, pltpu.roll(product[:PART], 1, 1))
    return total + jnp.where(lane == XD - 1, 0.0, pltpu.roll(product[2 * PART :], XD - 1, 1))


def sigmoid(x):
    return (1.0 / (1.0 + jnp.exp(-x))).astype(bf16)


def one_hot(line, count, value=None):
    rows = iota((count, line.shape[1]), 0).astype(f32).astype(bf16)
    return jnp.where(rows == line, jnp.ones((), bf16) if value is None else value, jnp.zeros((), bf16))


def pair_hot(line, count, first, second):
    return jnp.concatenate([one_hot(line, count, first), one_hot(line, count, second)], axis=0)


def small(x):
    return x.astype(f32).astype(bf16)


def split(number):
    q = ((number >> 5) * 171) >> 9
    return small((q & 3) * STEP + (q >> 2)), small(number - q * LOW)


def chunk_sums(chunks):
    a_parts = [pair_hot(row, HALF, value, cross) for row, _, value, cross in chunks]
    b_parts = [one_hot(column, LOW) for _, column, _, _ in chunks]
    return along(jnp.concatenate(a_parts, axis=1), jnp.concatenate(b_parts, axis=1))


def relaid(total):
    a, b, c, d = (total[j * STEP : (j + 1) * STEP] for j in range(4))
    return (
        jnp.concatenate([a, b[:, :32]], axis=1),
        jnp.concatenate([b[:, 32:], c[:, :64]], axis=1),
        jnp.concatenate([c[:, 64:], d], axis=1),
    )


def crossings(here, above):
    m, n = iota((ROWS, XD), 0), iota((ROWS, XD), 1)
    under_z = jnp.concatenate([here[:YD], here[:-YD]], axis=0)
    under_y = pltpu.roll(here, 1, 0)
    if above is not None:
        above = jnp.concatenate([jnp.broadcast_to(above[z : z + 1], (YD, XD)) for z in range(Z)], axis=0)
        under_y = jnp.where(m % YD == 0, above, under_y)
    under_x = jnp.where(n == 0, here, pltpu.roll(here, 1, 1))
    unders = (under_z, under_y, under_x)
    return jnp.concatenate([jnp.where((here != under) & (under > 0), 1.0, 0.0) for under in unders], axis=0)


def fill_pairs(logits, crossed, value, cross):
    n = iota(logits.shape, 1)
    crossed = jnp.where((n > 0) & (n < XD - 1), crossed, 0.0)
    cross[...] = crossed
    value[...] = crossed * sigmoid(logits).astype(f32)


def lines_of(i, rows, slots, value, cross):
    at = slice(i * YD, (i + 1) * YD)
    tiles = (*split(slots[at]), value[at].astype(bf16), cross[at].astype(bf16))
    return [[tile[j : j + 1] for tile in tiles] for j in rows]


def batched(chunks, size=BATCH):
    return sum(chunk_sums(chunks[i : i + size]) for i in range(0, len(chunks), size))


def inner_kernel(two, one, taps, logits, early, ids, slots, full, sums, ends, halo, value, cross):
    top, bottom = placed(one[...].astype(f32), two[...].astype(f32), "yx")
    halo[:CZ] = top[:CZ].astype(bf16)
    halo[CZ : 2 * CZ] = bottom[:CZ].astype(bf16)
    halo[2 * CZ :] = jnp.zeros((LANES - 2 * CZ, XD), bf16)
    total = logits[...] + shifted(jnp.dot(taps[:, CELLS:], halo[...], preferred_element_type=f32))
    full[...] = total
    above = top[CZ:]
    above = (above[:Z] * 128.0 + above[Z:]).astype(i32)
    crossed = crossings(ids[...], above)
    fill_pairs(total, crossed, value, cross)
    pad = jnp.zeros((XD - PART, XD), f32)
    numbers = slots[...]
    kinds = [crossed, (numbers >> 7).astype(f32), (numbers & 127).astype(f32)]
    rest = total
    for _ in range(3):
        kinds.append(rest.astype(bf16).astype(f32))
        rest = rest - kinds[-1]
    kinds = jnp.concatenate([part for kind in kinds for part in (kind, pad)], axis=0)
    picked = along(pick_ends(), kinds.astype(bf16))
    ends[:, : 3 * XD] = picked[:, : 3 * XD]
    ends[:, 3 * XD :] = picked[:, 3 * XD : 4 * XD] + picked[:, 4 * XD : 5 * XD] + picked[:, 5 * XD :]
    chunks = [line for i in range(1, EARLY) for line in lines_of(i, (0, YD - 1), slots, value, cross)]
    chunks += [line for i in range(EARLY, C_OUT * Z) for line in lines_of(i, range(YD), slots, value, cross)]
    sums[...] = early[...] + batched(chunks)


def end_rows(left, right):
    row = iota((8, DEPTH), 0)
    return jnp.where(row == 0, left[:, :DEPTH], jnp.where(row == 1, right[:, :DEPTH], 0.0)).astype(bf16)


def send_kernel(outer, inner, taps, own, ends, sums, bucket, outgoing):
    left, right = placed(inner[...], outer[...], "gz")
    both = end_rows(left, right)
    first = along(both, taps[:PART])[0:1] + ends[0:1, 3 * XD : 3 * XD + PART]
    last = along(both, taps[2 * PART :])[1:2] + ends[1:2, 3 * XD : 3 * XD + PART]
    soft = sigmoid(jnp.concatenate([first, last], axis=0)).astype(f32)
    soft = jnp.concatenate([soft, jnp.zeros((2, XD - PART), f32)], axis=1)

    beside = left[:, DEPTH : DEPTH + ROWS] * 128.0 + left[:, DEPTH + ROWS :]
    here = own[:, DEPTH : DEPTH + ROWS] * 128.0 + own[:, DEPTH + ROWS :]
    differs = jnp.where((beside != here) & (beside > 0.0), 1.0, 0.0)
    differs = jnp.concatenate([jnp.zeros((1, 2 * ROWS), f32), differs, jnp.zeros((1, XD - PART), f32)], axis=1)
    chunks = []
    for end in range(2):
        crossed = ends[end : end + 1, :XD]
        if end == 0:
            crossed = crossed + differs
        slot = ends[end : end + 1, XD : 2 * XD] * 128.0 + ends[end : end + 1, 2 * XD : 3 * XD]
        chunks.append((*split(slot.astype(i32)), (soft[end : end + 1] * crossed).astype(bf16), crossed.astype(bf16)))
    total = sums[...] + chunk_sums(chunks)
    kinds = [[part.astype(bf16) for part in relaid(total[at : at + HALF])] for at in (0, HALF)]
    owners, places = small(bucket[...] >> 6), small(bucket[...] & 63)
    a_parts, b_parts = [], []
    for h in range(HIGH):
        k, j = divmod(h, 3)
        a_parts.append(one_hot(owners[h : h + 1], LANES))
        b_parts.append(pair_hot(places[h : h + 1], BUCKET, kinds[0][j][k : k + 1], kinds[1][j][k : k + 1]))
    sent = along(jnp.concatenate(a_parts, axis=1), jnp.concatenate(b_parts, axis=1))
    outgoing[...] = sent


def affinity_kernel(outer, inner, taps, logits, affinity):
    both = end_rows(*placed(inner[...], outer[...], "gz"))
    first = along(taps[:PART], both)[:, 0:1]
    last = along(taps[2 * PART :], both)[:, 1:2]
    lane = iota((PART, XD), 1)
    ends = jnp.where(lane == 0, first, jnp.where(lane == XD - 1, last, 0.0))
    affinity[...] = sigmoid(logits[...] + ends)


def edges_kernel(arrived, rows, mean):
    n = arrived.shape[0]
    same = jnp.where(iota((n, n), 0) == iota((n, n), 1), 1.0, 0.0).astype(bf16)
    got = lax.dot_general(arrived[...].astype(bf16), same, (((0,), (0,)), ((), ())), preferred_element_type=f32)
    got = got.astype(bf16)
    row, column = split(rows[...])
    total = chunk_sums(
        [
            (row[q : q + 1], column[q : q + 1], got[q : q + 1], got[BUCKET + q : BUCKET + q + 1])
            for q in range(BUCKET)
        ]
    )
    parts = relaid(total[:HALF] / jnp.maximum(total[HALF:], 1.0))
    for h in range(HIGH):
        k, j = divmod(h, 3)
        mean[h : h + 1] = parts[j][k : k + 1]


def swapped(block, axis, first):
    pairs = [(i, i + 1) for i in range(first, lax.axis_size(axis) - 1, 2)]
    return held(lax.ppermute(block, axis, pairs + [(j, i) for i, j in pairs]))


def local(features, conv_weight, conv_bias, fragments, pair_slot, slot_bucket, arrival_row):
    devices = lax.axis_size("gz") * lax.axis_size("yx")
    inputs = (
        features.reshape(CELLS, XD),
        fragments.reshape(ROWS, XD),
        pair_slot.reshape(PART, XD),
        conv_weight.transpose(0, 2, 3, 4, 1).reshape(27, 3, C_IN),
        slot_bucket.reshape(HIGH, LANES),
        arrival_row[0].T,
        conv_bias.reshape(1, C_OUT),
    )
    pairs = [pltpu.VMEM((PART, XD), f32)] * 2
    sums_shape = near((2 * HALF, LOW), f32)
    lines = near((CZ + 2 * Z, XD), bf16)
    one, two, *inputs = pl.pallas_call(
        rows_kernel,
        out_shape=(lines, lines, *(near(x.shape, x.dtype) for x in inputs)),
        in_specs=[pl.BlockSpec(memory_space=pl.ANY)] * len(inputs),
        out_specs=tuple(whole(2 + len(inputs))),
        scratch_shapes=[pltpu.SemaphoreType.DMA((len(inputs),))],
    )(*inputs)
    cells, ids, slots, weights, bucket, targets, bias = map(held, inputs)
    two = swapped(two, "yx", 1)
    one = swapped(one, "yx", 0)
    taps, logits, early = pl.pallas_call(
        taps_kernel,
        out_shape=(near((TAP_ROWS, DEPTH), bf16), near((PART, XD), f32), sums_shape),
        in_specs=whole(5),
        out_specs=tuple(whole(3)),
        scratch_shapes=[pltpu.VMEM((27 * 8, LANES), f32)] + [pltpu.VMEM((EARLY * YD, XD), f32)] * 2,
    )(cells, weights, bias, ids, slots)
    taps, logits, early = held(taps), held(logits), held(early)
    inner, outer, own = pl.pallas_call(
        columns_kernel,
        out_shape=(near((1, WIDE), f32),) * 3,
        in_specs=whole(5),
        out_specs=tuple(whole(3)),
        scratch_shapes=[pltpu.VMEM((WIDE, XD), bf16)],
    )(two, one, cells, ids, early)
    outer = swapped(outer, "gz", 1)
    inner = swapped(inner, "gz", 0)
    logits, sums, ends = pl.pallas_call(
        inner_kernel,
        out_shape=(near((PART, XD), f32), sums_shape, near((8, 4 * XD), f32)),
        in_specs=whole(7),
        out_specs=tuple(whole(3)),
        scratch_shapes=[pltpu.VMEM((LANES, XD), bf16)] + pairs,
    )(two, one, taps, logits, early, ids, slots)
    logits = held(logits)
    outgoing = pl.pallas_call(
        send_kernel,
        out_shape=near((devices, 2 * BUCKET), f32),
        in_specs=whole(7),
        out_specs=whole(1)[0],
    )(outer, inner, taps, held(own), held(ends), held(sums), bucket)
    arrived = lax.all_to_all(held(outgoing), ("gz", "yx"), split_axis=0, concat_axis=0, tiled=True)
    affinity = pl.pallas_call(
        affinity_kernel,
        out_shape=jax.ShapeDtypeStruct((PART, XD), bf16),
        in_specs=whole(4),
        out_specs=whole(1)[0],
    )(outer, inner, taps, logits)
    mean = pl.pallas_call(
        edges_kernel,
        out_shape=jax.ShapeDtypeStruct((HIGH, LANES), f32),
        in_specs=whole(2),
        out_specs=whole(1)[0],
    )(held(arrived), targets)
    return affinity.reshape(C_OUT, Z, YD, XD), mean.reshape(E_OWN)


def solution(mesh):
    return jax.shard_map(
        local,
        mesh=mesh,
        in_specs=(
            P(None, None, "yx", "gz"),
            P(),
            P(),
            P(None, "yx", "gz"),
            P(None, None, "yx", "gz"),
            P(("gz", "yx"), None),
            P(("gz", "yx"), None, None),
        ),
        out_specs=(P(None, None, "yx", "gz"), P(("gz", "yx"))),
        check_vma=False,
    )
```

```python
import functools

import jax
import jax.numpy as jnp
from jax import lax
from jax.experimental import pallas as pl
from jax.experimental.pallas import tpu as pltpu
from jax.sharding import PartitionSpec as P

C_IN, C_OUT, Z, YD, XD = 12, 3, 4, 16, 256
BUCKET, E_OWN, P_LOC = 64, 4096, 4096
CZ = C_IN * Z
CELLS = CZ * YD
DEPTH = CELLS + 2 * CZ + 32
WIDE = DEPTH + 2 * Z * YD
ROWS = Z * YD
LANES = 128
HIGH = P_LOC // LANES

TAP_ROWS = 9 * ROWS
PART = C_OUT * ROWS
EARLY = 9
BATCH = 48
LOW, HALF, STEP = 96, 48, 12

f32, bf16, i32 = jnp.float32, jnp.bfloat16, jnp.int32


def iota(shape, dim):
    return lax.broadcasted_iota(i32, shape, dim)


def along(a, b):
    return lax.dot_general(a, b, (((1,), (1,)), ((), ())), preferred_element_type=f32)


def whole(count):
    return [pl.BlockSpec(memory_space=pltpu.VMEM)] * count


def near(shape, dtype):
    return pltpu.VMEM(shape, dtype)


def held(x):
    return pltpu.with_memory_space_constraint(x, pltpu.VMEM)


def even(axis):
    return lax.rem(lax.axis_index(axis), 2) == 0


def rows_kernel(*refs):
    count = len(refs) // 2 - 1
    sources, (one, two), held_refs, sems = refs[:count], refs[count : count + 2], refs[count + 2 : -1], refs[-1]
    copies = [pltpu.make_async_copy(a, b, sems.at[i]) for i, (a, b) in enumerate(zip(sources, held_refs))]
    for copy in copies:
        copy.start()
    cells, ids = held_refs[:2]
    row = iota((2 * CZ, CELLS), 0)
    inner = jnp.where(even("yx"), YD - 1, 0)
    wanted = jnp.where(row < CZ, row * YD + inner, (row - CZ) * YD + (YD - 1 - inner))
    pick = jnp.where(iota((2 * CZ, CELLS), 1) == wanted, 1.0, 0.0).astype(bf16)
    copies[0].wait()
    picked = jnp.dot(pick, cells[...], preferred_element_type=f32).astype(bf16)
    copies[1].wait()
    last = jnp.concatenate([ids[(z + 1) * YD - 1 : (z + 1) * YD] for z in range(Z)], axis=0)
    pair = jnp.concatenate([last >> 7, last & 127], axis=0).astype(f32).astype(bf16)
    one[:CZ] = picked[:CZ]
    two[:CZ] = picked[CZ:]
    one[CZ:] = pair
    two[CZ:] = pair
    for copy in copies[2:]:
        copy.wait()


def placed(inner, outer, axis):
    at, last, first = lax.axis_index(axis), lax.axis_size(axis) - 1, even(axis)
    before, after = jnp.where(first, outer, inner), jnp.where(first, inner, outer)
    zero = jnp.zeros((), before.dtype)
    return jnp.where(at == 0, zero, before), jnp.where(at == last, zero, after)


def pick_ends():
    row, lane = iota((8, XD), 0), iota((8, XD), 1)
    return jnp.where((row < 2) & (lane == row * (XD - 1)), 1.0, 0.0).astype(bf16)


def columns_kernel(two, one, cells, ids, after, inner, outer, own, wide):
    top, bottom = placed(one[:CZ], two[:CZ], "yx")
    wide[:CELLS] = cells[...]
    wide[CELLS : CELLS + CZ] = top
    wide[CELLS + CZ : CELLS + 2 * CZ] = bottom
    wide[CELLS + 2 * CZ : DEPTH] = jnp.zeros((DEPTH - CELLS - 2 * CZ, XD), bf16)
    wide[DEPTH : DEPTH + ROWS] = (ids[...] >> 7).astype(f32).astype(bf16)
    wide[DEPTH + ROWS :] = (ids[...] & 127).astype(f32).astype(bf16)
    picked = along(pick_ends(), wide[...])
    first = even("gz")
    inner[...] = jnp.where(first, picked[1:2], picked[0:1])
    outer[...] = jnp.where(first, picked[0:1], picked[1:2])
    own[...] = picked[0:1]


def taps_kernel(cells, weights, bias, ids, slots, taps, logits, sums, flat, value, cross):
    flat[...] = jnp.zeros(flat.shape, f32)
    for i in range(27):
        flat[8 * i : 8 * i + 3, :C_IN] = weights[i].astype(f32)
    k = iota((LANES, DEPTH), 1)
    channel = jnp.where(k < CELLS, k // (Z * YD), ((k - CELLS) % CZ) // Z)
    channel = jnp.where(k < CELLS + 2 * CZ, channel, LANES)
    spread = jnp.where(iota((LANES, DEPTH), 0) == channel, 1.0, 0.0).astype(bf16)
    lines = jnp.dot(flat[...].astype(bf16), spread, preferred_element_type=f32).astype(bf16)
    for t in range(DEPTH // LANES):
        y, k = iota((YD, LANES), 0), iota((YD, LANES), 1) + t * LANES
        inner = k < CELLS
        z_in = small(jnp.where(inner, (k // YD) % Z, (k - CELLS) % Z))
        y_in = jnp.where(inner, k % YD, jnp.where(k < CELLS + CZ, -1, YD))
        y_in = jnp.where(k < CELLS + 2 * CZ, y_in, 3 * YD)
        dy = small(y_in - y + 1)
        for e in range(3):
            for o in range(C_OUT):
                bands = []
                for a in range(3):
                    band = jnp.zeros((YD, LANES), bf16)
                    for b in range(3):
                        r = (o * 9 + a * 3 + b) * 8 + e
                        band = jnp.where(dy == float(b), lines[r : r + 1, t * LANES : (t + 1) * LANES], band)
                    bands.append(band)
                for z in range(Z):
                    tap = jnp.zeros((YD, LANES), bf16)
                    for a in range(3):
                        if 0 <= z + a - 1 < Z:
                            tap = jnp.where(z_in == float(z + a - 1), bands[a], tap)
                    row = ((e * C_OUT + o) * Z + z) * YD
                    taps[row : row + YD, t * LANES : (t + 1) * LANES] = tap
    product = jnp.dot(taps[:, :CELLS], cells[...], preferred_element_type=f32)
    offset = jnp.concatenate([jnp.broadcast_to(bias[:, o : o + 1], (ROWS, 1)) for o in range(C_OUT)], axis=0)
    total = shifted(product) + offset
    logits[...] = total
    rows = EARLY * YD
    fill_pairs(total[:rows], crossings(ids[...], None)[:rows], value, cross)
    sums[...] = batched([line for i in range(1, EARLY) for line in lines_of(i, range(1, YD - 1), slots, value, cross)])


def shifted(product):
    lane = iota((PART, XD), 1)
    total = product[PART : 2 * PART]
    total += jnp.where(lane == 0, 0.0, pltpu.roll(product[:PART], 1, 1))
    return total + jnp.where(lane == XD - 1, 0.0, pltpu.roll(product[2 * PART :], XD - 1, 1))


def sigmoid(x):
    return (1.0 / (1.0 + jnp.exp(-x))).astype(bf16)


def one_hot(line, count, value=None):
    rows = iota((count, line.shape[1]), 0).astype(f32).astype(bf16)
    return jnp.where(rows == line, jnp.ones((), bf16) if value is None else value, jnp.zeros((), bf16))


def pair_hot(line, count, first, second):
    return jnp.concatenate([one_hot(line, count, first), one_hot(line, count, second)], axis=0)


def small(x):
    return x.astype(f32).astype(bf16)


def split(number):
    q = ((number >> 5) * 171) >> 9
    return small((q & 3) * STEP + (q >> 2)), small(number - q * LOW)


def chunk_sums(chunks):
    a_parts = [pair_hot(row, HALF, value, cross) for row, _, value, cross in chunks]
    b_parts = [one_hot(column, LOW) for _, column, _, _ in chunks]
    return along(jnp.concatenate(a_parts, axis=1), jnp.concatenate(b_parts, axis=1))


def relaid(total):
    a, b, c, d = (total[j * STEP : (j + 1) * STEP] for j in range(4))
    return (
        jnp.concatenate([a, b[:, :32]], axis=1),
        jnp.concatenate([b[:, 32:], c[:, :64]], axis=1),
        jnp.concatenate([c[:, 64:], d], axis=1),
    )


def crossings(here, above):
    m, n = iota((ROWS, XD), 0), iota((ROWS, XD), 1)
    under_z = jnp.concatenate([here[:YD], here[:-YD]], axis=0)
    under_y = pltpu.roll(here, 1, 0)
    if above is not None:
        above = jnp.concatenate([jnp.broadcast_to(above[z : z + 1], (YD, XD)) for z in range(Z)], axis=0)
        under_y = jnp.where(m % YD == 0, above, under_y)
    under_x = jnp.where(n == 0, here, pltpu.roll(here, 1, 1))
    unders = (under_z, under_y, under_x)
    return jnp.concatenate([jnp.where((here != under) & (under > 0), 1.0, 0.0) for under in unders], axis=0)


def fill_pairs(logits, crossed, value, cross):
    n = iota(logits.shape, 1)
    crossed = jnp.where((n > 0) & (n < XD - 1), crossed, 0.0)
    cross[...] = crossed
    value[...] = crossed * sigmoid(logits).astype(f32)


def lines_of(i, rows, slots, value, cross):
    at = slice(i * YD, (i + 1) * YD)
    tiles = (*split(slots[at]), value[at].astype(bf16), cross[at].astype(bf16))
    return [[tile[j : j + 1] for tile in tiles] for j in rows]


def batched(chunks, size=BATCH):
    return sum(chunk_sums(chunks[i : i + size]) for i in range(0, len(chunks), size))


def inner_kernel(two, one, taps, logits, early, ids, slots, full, sums, ends, halo, value, cross):
    top, bottom = placed(one[...].astype(f32), two[...].astype(f32), "yx")
    halo[:CZ] = top[:CZ].astype(bf16)
    halo[CZ : 2 * CZ] = bottom[:CZ].astype(bf16)
    halo[2 * CZ :] = jnp.zeros((LANES - 2 * CZ, XD), bf16)
    total = logits[...] + shifted(jnp.dot(taps[:, CELLS:], halo[...], preferred_element_type=f32))
    full[...] = total
    above = top[CZ:]
    above = (above[:Z] * 128.0 + above[Z:]).astype(i32)
    crossed = crossings(ids[...], above)
    fill_pairs(total, crossed, value, cross)
    pad = jnp.zeros((XD - PART, XD), f32)
    numbers = slots[...]
    kinds = [crossed, (numbers >> 7).astype(f32), (numbers & 127).astype(f32)]
    rest = total
    for _ in range(3):
        kinds.append(rest.astype(bf16).astype(f32))
        rest = rest - kinds[-1]
    kinds = jnp.concatenate([part for kind in kinds for part in (kind, pad)], axis=0)
    picked = along(pick_ends(), kinds.astype(bf16))
    ends[:, : 3 * XD] = picked[:, : 3 * XD]
    ends[:, 3 * XD :] = picked[:, 3 * XD : 4 * XD] + picked[:, 4 * XD : 5 * XD] + picked[:, 5 * XD :]
    chunks = [line for i in range(1, EARLY) for line in lines_of(i, (0, YD - 1), slots, value, cross)]
    chunks += [line for i in range(EARLY, C_OUT * Z) for line in lines_of(i, range(YD), slots, value, cross)]
    sums[...] = early[...] + batched(chunks)


def end_rows(left, right):
    row = iota((8, DEPTH), 0)
    return jnp.where(row == 0, left[:, :DEPTH], jnp.where(row == 1, right[:, :DEPTH], 0.0)).astype(bf16)


def send_kernel(outer, inner, taps, own, ends, sums, bucket, outgoing):
    left, right = placed(inner[...], outer[...], "gz")
    both = end_rows(left, right)
    first = along(both, taps[:PART])[0:1] + ends[0:1, 3 * XD : 3 * XD + PART]
    last = along(both, taps[2 * PART :])[1:2] + ends[1:2, 3 * XD : 3 * XD + PART]
    soft = sigmoid(jnp.concatenate([first, last], axis=0)).astype(f32)
    soft = jnp.concatenate([soft, jnp.zeros((2, XD - PART), f32)], axis=1)

    beside = left[:, DEPTH : DEPTH + ROWS] * 128.0 + left[:, DEPTH + ROWS :]
    here = own[:, DEPTH : DEPTH + ROWS] * 128.0 + own[:, DEPTH + ROWS :]
    differs = jnp.where((beside != here) & (beside > 0.0), 1.0, 0.0)
    differs = jnp.concatenate([jnp.zeros((1, 2 * ROWS), f32), differs, jnp.zeros((1, XD - PART), f32)], axis=1)
    chunks = []
    for end in range(2):
        crossed = ends[end : end + 1, :XD]
        if end == 0:
            crossed = crossed + differs
        slot = ends[end : end + 1, XD : 2 * XD] * 128.0 + ends[end : end + 1, 2 * XD : 3 * XD]
        chunks.append((*split(slot.astype(i32)), (soft[end : end + 1] * crossed).astype(bf16), crossed.astype(bf16)))
    total = sums[...] + chunk_sums(chunks)
    kinds = [[part.astype(bf16) for part in relaid(total[at : at + HALF])] for at in (0, HALF)]
    owners, places = small(bucket[...] >> 6), small(bucket[...] & 63)
    a_parts, b_parts = [], []
    for h in range(HIGH):
        k, j = divmod(h, 3)
        a_parts.append(one_hot(owners[h : h + 1], LANES))
        b_parts.append(pair_hot(places[h : h + 1], BUCKET, kinds[0][j][k : k + 1], kinds[1][j][k : k + 1]))
    sent = along(jnp.concatenate(a_parts, axis=1), jnp.concatenate(b_parts, axis=1))
    outgoing[...] = sent


def affinity_kernel(outer, inner, taps, logits, affinity):
    both = end_rows(*placed(inner[...], outer[...], "gz"))
    first = along(taps[:PART], both)[:, 0:1]
    last = along(taps[2 * PART :], both)[:, 1:2]
    lane = iota((PART, XD), 1)
    ends = jnp.where(lane == 0, first, jnp.where(lane == XD - 1, last, 0.0))
    affinity[...] = sigmoid(logits[...] + ends)


def edges_kernel(arrived, rows, mean):
    n = arrived.shape[0]
    same = jnp.where(iota((n, n), 0) == iota((n, n), 1), 1.0, 0.0).astype(bf16)
    got = lax.dot_general(arrived[...].astype(bf16), same, (((0,), (0,)), ((), ())), preferred_element_type=f32)
    got = got.astype(bf16)
    row, column = split(rows[...])
    total = chunk_sums(
        [
            (row[q : q + 1], column[q : q + 1], got[q : q + 1], got[BUCKET + q : BUCKET + q + 1])
            for q in range(BUCKET)
        ]
    )
    parts = relaid(total[:HALF] / jnp.maximum(total[HALF:], 1.0))
    for h in range(HIGH):
        k, j = divmod(h, 3)
        mean[h : h + 1] = parts[j][k : k + 1]


def swapped(block, axis, first, ring=False):
    size = lax.axis_size(axis)
    other = [i + 1 if (i - first) % 2 == 0 else i - 1 for i in range(size)]
    if ring:
        other = [i % size for i in other]
    else:
        other = [j if 0 <= j < size else i for i, j in enumerate(other)]
    return held(lax.ppermute(block, axis, list(enumerate(other))))


def local(features, conv_weight, conv_bias, fragments, pair_slot, slot_bucket, arrival_row):
    devices = lax.axis_size("gz") * lax.axis_size("yx")
    inputs = (
        features.reshape(CELLS, XD),
        fragments.reshape(ROWS, XD),
        pair_slot.reshape(PART, XD),
        conv_weight.transpose(0, 2, 3, 4, 1).reshape(27, 3, C_IN),
        slot_bucket.reshape(HIGH, LANES),
        arrival_row[0].T,
        conv_bias.reshape(1, C_OUT),
    )
    pairs = [pltpu.VMEM((PART, XD), f32)] * 2
    sums_shape = near((2 * HALF, LOW), f32)
    lines = near((CZ + 2 * Z, XD), bf16)
    one, two, *inputs = pl.pallas_call(
        rows_kernel,
        out_shape=(lines, lines, *(near(x.shape, x.dtype) for x in inputs)),
        in_specs=[pl.BlockSpec(memory_space=pl.ANY)] * len(inputs),
        out_specs=tuple(whole(2 + len(inputs))),
        scratch_shapes=[pltpu.SemaphoreType.DMA((len(inputs),))],
    )(*inputs)
    cells, ids, slots, weights, bucket, targets, bias = map(held, inputs)
    two = swapped(two, "yx", 1, ring=True)
    one = swapped(one, "yx", 0)
    taps, logits, early = pl.pallas_call(
        taps_kernel,
        out_shape=(near((TAP_ROWS, DEPTH), bf16), near((PART, XD), f32), sums_shape),
        in_specs=whole(5),
        out_specs=tuple(whole(3)),
        scratch_shapes=[pltpu.VMEM((27 * 8, LANES), f32)] + [pltpu.VMEM((EARLY * YD, XD), f32)] * 2,
    )(cells, weights, bias, ids, slots)
    taps, logits, early = held(taps), held(logits), held(early)
    inner, outer, own = pl.pallas_call(
        columns_kernel,
        out_shape=(near((1, WIDE), f32),) * 3,
        in_specs=whole(5),
        out_specs=tuple(whole(3)),
        scratch_shapes=[pltpu.VMEM((WIDE, XD), bf16)],
    )(two, one, cells, ids, early)
    outer = swapped(outer, "gz", 1, ring=True)
    inner = swapped(inner, "gz", 0)
    logits, sums, ends = pl.pallas_call(
        inner_kernel,
        out_shape=(near((PART, XD), f32), sums_shape, near((8, 4 * XD), f32)),
        in_specs=whole(7),
        out_specs=tuple(whole(3)),
        scratch_shapes=[pltpu.VMEM((LANES, XD), bf16)] + pairs,
    )(two, one, taps, logits, early, ids, slots)
    logits = held(logits)
    outgoing = pl.pallas_call(
        send_kernel,
        out_shape=near((devices, 2 * BUCKET), f32),
        in_specs=whole(7),
        out_specs=whole(1)[0],
    )(outer, inner, taps, held(own), held(ends), held(sums), bucket)
    arrived = lax.all_to_all(held(outgoing), ("gz", "yx"), split_axis=0, concat_axis=0, tiled=True)
    affinity = pl.pallas_call(
        affinity_kernel,
        out_shape=jax.ShapeDtypeStruct((PART, XD), bf16),
        in_specs=whole(4),
        out_specs=whole(1)[0],
    )(outer, inner, taps, logits)
    mean = pl.pallas_call(
        edges_kernel,
        out_shape=jax.ShapeDtypeStruct((HIGH, LANES), f32),
        in_specs=whole(2),
        out_specs=whole(1)[0],
    )(held(arrived), targets)
    return affinity.reshape(C_OUT, Z, YD, XD), mean.reshape(E_OWN)


def solution(mesh):
    return jax.shard_map(
        local,
        mesh=mesh,
        in_specs=(
            P(None, None, "yx", "gz"),
            P(),
            P(),
            P(None, "yx", "gz"),
            P(None, None, "yx", "gz"),
            P(("gz", "yx"), None),
            P(("gz", "yx"), None, None),
        ),
        out_specs=(P(None, None, "yx", "gz"), P(("gz", "yx"))),
        check_vma=False,
    )
```

```python
import functools

import jax
import jax.numpy as jnp
from jax import lax
from jax.experimental import pallas as pl
from jax.experimental.pallas import tpu as pltpu
from jax.sharding import PartitionSpec as P

C_IN, C_OUT, Z, YD, XD = 12, 3, 4, 16, 256
BUCKET, E_OWN, P_LOC = 64, 4096, 4096
CZ = C_IN * Z
CELLS = CZ * YD
DEPTH = CELLS + 2 * CZ + 32
WIDE = DEPTH + 2 * Z * YD
ROWS = Z * YD
LANES = 128
HIGH = P_LOC // LANES

TAP_ROWS = 9 * ROWS
PART = C_OUT * ROWS
EARLY = 9
BATCH = 48
LOW, HALF, STEP = 96, 48, 12

f32, bf16, i32 = jnp.float32, jnp.bfloat16, jnp.int32


def iota(shape, dim):
    return lax.broadcasted_iota(i32, shape, dim)


def along(a, b):
    return lax.dot_general(a, b, (((1,), (1,)), ((), ())), preferred_element_type=f32)


def whole(count):
    return [pl.BlockSpec(memory_space=pltpu.VMEM)] * count


def near(shape, dtype):
    return pltpu.VMEM(shape, dtype)


def held(x):
    return pltpu.with_memory_space_constraint(x, pltpu.VMEM)


def even(axis):
    return lax.rem(lax.axis_index(axis), 2) == 0


def rows_kernel(*refs):
    count = len(refs) // 2 - 1
    sources, (one, two), held_refs, sems = refs[:count], refs[count : count + 2], refs[count + 2 : -1], refs[-1]
    copies = [pltpu.make_async_copy(a, b, sems.at[i]) for i, (a, b) in enumerate(zip(sources, held_refs))]
    for copy in copies:
        copy.start()
    cells, ids = held_refs[:2]
    row = iota((2 * CZ, CELLS), 0)
    inner = jnp.where(even("yx"), YD - 1, 0)
    wanted = jnp.where(row < CZ, row * YD + inner, (row - CZ) * YD + (YD - 1 - inner))
    pick = jnp.where(iota((2 * CZ, CELLS), 1) == wanted, 1.0, 0.0).astype(bf16)
    copies[0].wait()
    picked = jnp.dot(pick, cells[...], preferred_element_type=f32).astype(bf16)
    copies[1].wait()
    last = jnp.concatenate([ids[(z + 1) * YD - 1 : (z + 1) * YD] for z in range(Z)], axis=0)
    pair = jnp.concatenate([last >> 7, last & 127], axis=0).astype(f32).astype(bf16)
    one[:CZ] = picked[:CZ]
    two[:CZ] = picked[CZ:]
    one[CZ:] = pair
    two[CZ:] = pair
    for copy in copies[2:]:
        copy.wait()


def placed(inner, outer, axis):
    at, last, first = lax.axis_index(axis), lax.axis_size(axis) - 1, even(axis)
    before, after = jnp.where(first, outer, inner), jnp.where(first, inner, outer)
    zero = jnp.zeros((), before.dtype)
    return jnp.where(at == 0, zero, before), jnp.where(at == last, zero, after)


def pick_ends():
    row, lane = iota((8, XD), 0), iota((8, XD), 1)
    return jnp.where((row < 2) & (lane == row * (XD - 1)), 1.0, 0.0).astype(bf16)


def columns_kernel(two, one, cells, ids, after, inner, outer, own, wide):
    top, bottom = placed(one[:CZ], two[:CZ], "yx")
    wide[:CELLS] = cells[...]
    wide[CELLS : CELLS + CZ] = top
    wide[CELLS + CZ : CELLS + 2 * CZ] = bottom
    wide[CELLS + 2 * CZ : DEPTH] = jnp.zeros((DEPTH - CELLS - 2 * CZ, XD), bf16)
    wide[DEPTH : DEPTH + ROWS] = (ids[...] >> 7).astype(f32).astype(bf16)
    wide[DEPTH + ROWS :] = (ids[...] & 127).astype(f32).astype(bf16)
    picked = along(pick_ends(), wide[...])
    first = even("gz")
    inner[...] = jnp.where(first, picked[1:2], picked[0:1])
    outer[...] = jnp.where(first, picked[0:1], picked[1:2])
    own[...] = picked[0:1]


def taps_kernel(cells, weights, bias, ids, slots, taps, logits, sums, flat, value, cross):
    flat[...] = jnp.zeros(flat.shape, f32)
    for i in range(27):
        flat[8 * i : 8 * i + 3, :C_IN] = weights[i].astype(f32)
    k = iota((LANES, DEPTH), 1)
    channel = jnp.where(k < CELLS, k // (Z * YD), ((k - CELLS) % CZ) // Z)
    channel = jnp.where(k < CELLS + 2 * CZ, channel, LANES)
    spread = jnp.where(iota((LANES, DEPTH), 0) == channel, 1.0, 0.0).astype(bf16)
    lines = jnp.dot(flat[...].astype(bf16), spread, preferred_element_type=f32).astype(bf16)
    for t in range(DEPTH // LANES):
        y, k = iota((YD, LANES), 0), iota((YD, LANES), 1) + t * LANES
        inner = k < CELLS
        z_in = small(jnp.where(inner, (k // YD) % Z, (k - CELLS) % Z))
        y_in = jnp.where(inner, k % YD, jnp.where(k < CELLS + CZ, -1, YD))
        y_in = jnp.where(k < CELLS + 2 * CZ, y_in, 3 * YD)
        dy = small(y_in - y + 1)
        for e in range(3):
            for o in range(C_OUT):
                bands = []
                for a in range(3):
                    band = jnp.zeros((YD, LANES), bf16)
                    for b in range(3):
                        r = (o * 9 + a * 3 + b) * 8 + e
                        band = jnp.where(dy == float(b), lines[r : r + 1, t * LANES : (t + 1) * LANES], band)
                    bands.append(band)
                for z in range(Z):
                    tap = jnp.zeros((YD, LANES), bf16)
                    for a in range(3):
                        if 0 <= z + a - 1 < Z:
                            tap = jnp.where(z_in == float(z + a - 1), bands[a], tap)
                    row = ((e * C_OUT + o) * Z + z) * YD
                    taps[row : row + YD, t * LANES : (t + 1) * LANES] = tap
    product = jnp.dot(taps[:, :CELLS], cells[...], preferred_element_type=f32)
    offset = jnp.concatenate([jnp.broadcast_to(bias[:, o : o + 1], (ROWS, 1)) for o in range(C_OUT)], axis=0)
    total = shifted(product) + offset
    logits[...] = total
    rows = EARLY * YD
    fill_pairs(total[:rows], crossings(ids[...], None)[:rows], value, cross)
    sums[...] = batched([line for i in range(1, EARLY) for line in lines_of(i, range(1, YD - 1), slots, value, cross)])


def shifted(product):
    lane = iota((PART, XD), 1)
    total = product[PART : 2 * PART]
    total += jnp.where(lane == 0, 0.0, pltpu.roll(product[:PART], 1, 1))
    return total + jnp.where(lane == XD - 1, 0.0, pltpu.roll(product[2 * PART :], XD - 1, 1))


def sigmoid(x):
    return (1.0 / (1.0 + jnp.exp(-x))).astype(bf16)


def one_hot(line, count, value=None):
    rows = iota((count, line.shape[1]), 0).astype(f32).astype(bf16)
    return jnp.where(rows == line, jnp.ones((), bf16) if value is None else value, jnp.zeros((), bf16))


def pair_hot(line, count, first, second):
    return jnp.concatenate([one_hot(line, count, first), one_hot(line, count, second)], axis=0)


def small(x):
    return x.astype(f32).astype(bf16)


def split(number):
    q = ((number >> 5) * 171) >> 9
    return small((q & 3) * STEP + (q >> 2)), small(number - q * LOW)


def chunk_sums(chunks):
    a_parts = [pair_hot(row, HALF, value, cross) for row, _, value, cross in chunks]
    b_parts = [one_hot(column, LOW) for _, column, _, _ in chunks]
    return along(jnp.concatenate(a_parts, axis=1), jnp.concatenate(b_parts, axis=1))


def relaid(total):
    a, b, c, d = (total[j * STEP : (j + 1) * STEP] for j in range(4))
    return (
        jnp.concatenate([a, b[:, :32]], axis=1),
        jnp.concatenate([b[:, 32:], c[:, :64]], axis=1),
        jnp.concatenate([c[:, 64:], d], axis=1),
    )


def crossings(here, above):
    m, n = iota((ROWS, XD), 0), iota((ROWS, XD), 1)
    under_z = jnp.concatenate([here[:YD], here[:-YD]], axis=0)
    under_y = pltpu.roll(here, 1, 0)
    if above is not None:
        above = jnp.concatenate([jnp.broadcast_to(above[z : z + 1], (YD, XD)) for z in range(Z)], axis=0)
        under_y = jnp.where(m % YD == 0, above, under_y)
    under_x = jnp.where(n == 0, here, pltpu.roll(here, 1, 1))
    unders = (under_z, under_y, under_x)
    return jnp.concatenate([jnp.where((here != under) & (under > 0), 1.0, 0.0) for under in unders], axis=0)


def fill_pairs(logits, crossed, value, cross):
    n = iota(logits.shape, 1)
    crossed = jnp.where((n > 0) & (n < XD - 1), crossed, 0.0)
    cross[...] = crossed
    value[...] = crossed * sigmoid(logits).astype(f32)


def lines_of(i, rows, slots, value, cross):
    at = slice(i * YD, (i + 1) * YD)
    tiles = (*split(slots[at]), value[at].astype(bf16), cross[at].astype(bf16))
    return [[tile[j : j + 1] for tile in tiles] for j in rows]


def batched(chunks, size=BATCH):
    return sum(chunk_sums(chunks[i : i + size]) for i in range(0, len(chunks), size))


def inner_kernel(two, one, taps, logits, early, ids, slots, full, sums, ends, halo, value, cross):
    top, bottom = placed(one[...].astype(f32), two[...].astype(f32), "yx")
    halo[:CZ] = top[:CZ].astype(bf16)
    halo[CZ : 2 * CZ] = bottom[:CZ].astype(bf16)
    halo[2 * CZ :] = jnp.zeros((LANES - 2 * CZ, XD), bf16)
    total = logits[...] + shifted(jnp.dot(taps[:, CELLS:], halo[...], preferred_element_type=f32))
    full[...] = total
    above = top[CZ:]
    above = (above[:Z] * 128.0 + above[Z:]).astype(i32)
    crossed = crossings(ids[...], above)
    fill_pairs(total, crossed, value, cross)
    pad = jnp.zeros((XD - PART, XD), f32)
    numbers = slots[...]
    kinds = [crossed, (numbers >> 7).astype(f32), (numbers & 127).astype(f32)]
    rest = total
    for _ in range(3):
        kinds.append(rest.astype(bf16).astype(f32))
        rest = rest - kinds[-1]
    kinds = jnp.concatenate([part for kind in kinds for part in (kind, pad)], axis=0)
    picked = along(pick_ends(), kinds.astype(bf16))
    ends[:, : 3 * XD] = picked[:, : 3 * XD]
    ends[:, 3 * XD :] = picked[:, 3 * XD : 4 * XD] + picked[:, 4 * XD : 5 * XD] + picked[:, 5 * XD :]
    chunks = [line for i in range(1, EARLY) for line in lines_of(i, (0, YD - 1), slots, value, cross)]
    chunks += [line for i in range(EARLY, C_OUT * Z) for line in lines_of(i, range(YD), slots, value, cross)]
    sums[...] = early[...] + batched(chunks)


def end_rows(left, right):
    row = iota((8, DEPTH), 0)
    return jnp.where(row == 0, left[:, :DEPTH], jnp.where(row == 1, right[:, :DEPTH], 0.0)).astype(bf16)


def send_kernel(outer, inner, taps, own, ends, sums, bucket, outgoing):
    left, right = placed(inner[...], outer[...], "gz")
    both = end_rows(left, right)
    first = along(both, taps[:PART])[0:1] + ends[0:1, 3 * XD : 3 * XD + PART]
    last = along(both, taps[2 * PART :])[1:2] + ends[1:2, 3 * XD : 3 * XD + PART]
    soft = sigmoid(jnp.concatenate([first, last], axis=0)).astype(f32)
    soft = jnp.concatenate([soft, jnp.zeros((2, XD - PART), f32)], axis=1)

    beside = left[:, DEPTH : DEPTH + ROWS] * 128.0 + left[:, DEPTH + ROWS :]
    here = own[:, DEPTH : DEPTH + ROWS] * 128.0 + own[:, DEPTH + ROWS :]
    differs = jnp.where((beside != here) & (beside > 0.0), 1.0, 0.0)
    differs = jnp.concatenate([jnp.zeros((1, 2 * ROWS), f32), differs, jnp.zeros((1, XD - PART), f32)], axis=1)
    chunks = []
    for end in range(2):
        crossed = ends[end : end + 1, :XD]
        if end == 0:
            crossed = crossed + differs
        slot = ends[end : end + 1, XD : 2 * XD] * 128.0 + ends[end : end + 1, 2 * XD : 3 * XD]
        chunks.append((*split(slot.astype(i32)), (soft[end : end + 1] * crossed).astype(bf16), crossed.astype(bf16)))
    total = sums[...] + chunk_sums(chunks)
    kinds = [[part.astype(bf16) for part in relaid(total[at : at + HALF])] for at in (0, HALF)]
    owners, places = small(bucket[...] >> 6), small(bucket[...] & 63)
    a_parts, b_parts = [], []
    for h in range(HIGH):
        k, j = divmod(h, 3)
        a_parts.append(one_hot(owners[h : h + 1], LANES))
        b_parts.append(pair_hot(places[h : h + 1], BUCKET, kinds[0][j][k : k + 1], kinds[1][j][k : k + 1]))
    sent = along(jnp.concatenate(a_parts, axis=1), jnp.concatenate(b_parts, axis=1))
    outgoing[...] = sent


def affinity_kernel(outer, inner, taps, logits, affinity):
    both = end_rows(*placed(inner[...], outer[...], "gz"))
    first = along(taps[:PART], both)[:, 0:1]
    last = along(taps[2 * PART :], both)[:, 1:2]
    lane = iota((PART, XD), 1)
    ends = jnp.where(lane == 0, first, jnp.where(lane == XD - 1, last, 0.0))
    affinity[...] = sigmoid(logits[...] + ends)


def edges_kernel(arrived, rows, mean):
    n = arrived.shape[0]
    same = jnp.where(iota((n, n), 0) == iota((n, n), 1), 1.0, 0.0).astype(bf16)
    got = lax.dot_general(arrived[...].astype(bf16), same, (((0,), (0,)), ((), ())), preferred_element_type=f32)
    got = got.astype(bf16)
    row, column = split(rows[...])
    total = chunk_sums(
        [
            (row[q : q + 1], column[q : q + 1], got[q : q + 1], got[BUCKET + q : BUCKET + q + 1])
            for q in range(BUCKET)
        ]
    )
    parts = relaid(total[:HALF] / jnp.maximum(total[HALF:], 1.0))
    for h in range(HIGH):
        k, j = divmod(h, 3)
        mean[h : h + 1] = parts[j][k : k + 1]


def swapped(block, axis, first):
    gz, yx = lax.axis_size("gz"), lax.axis_size("yx")
    pairs = []
    for g in range(gz):
        for y in range(yx):
            at, size = (g, gz) if axis == "gz" else (y, yx)
            to = at + 1 if (at - first) % 2 == 0 else at - 1
            if not 0 <= to < size:
                g_to, y_to = (g, y ^ 1) if axis == "gz" else (g ^ 1, y)
            else:
                g_to, y_to = (to, y) if axis == "gz" else (g, to)
            pairs.append((g * yx + y, g_to * yx + y_to))
    return held(lax.ppermute(block, ("gz", "yx"), pairs))


def local(features, conv_weight, conv_bias, fragments, pair_slot, slot_bucket, arrival_row):
    devices = lax.axis_size("gz") * lax.axis_size("yx")
    inputs = (
        features.reshape(CELLS, XD),
        fragments.reshape(ROWS, XD),
        pair_slot.reshape(PART, XD),
        conv_weight.transpose(0, 2, 3, 4, 1).reshape(27, 3, C_IN),
        slot_bucket.reshape(HIGH, LANES),
        arrival_row[0].T,
        conv_bias.reshape(1, C_OUT),
    )
    pairs = [pltpu.VMEM((PART, XD), f32)] * 2
    sums_shape = near((2 * HALF, LOW), f32)
    lines = near((CZ + 2 * Z, XD), bf16)
    one, two, *inputs = pl.pallas_call(
        rows_kernel,
        out_shape=(lines, lines, *(near(x.shape, x.dtype) for x in inputs)),
        in_specs=[pl.BlockSpec(memory_space=pl.ANY)] * len(inputs),
        out_specs=tuple(whole(2 + len(inputs))),
        scratch_shapes=[pltpu.SemaphoreType.DMA((len(inputs),))],
    )(*inputs)
    cells, ids, slots, weights, bucket, targets, bias = map(held, inputs)
    two = swapped(two, "yx", 1)
    one = swapped(one, "yx", 0)
    taps, logits, early = pl.pallas_call(
        taps_kernel,
        out_shape=(near((TAP_ROWS, DEPTH), bf16), near((PART, XD), f32), sums_shape),
        in_specs=whole(5),
        out_specs=tuple(whole(3)),
        scratch_shapes=[pltpu.VMEM((27 * 8, LANES), f32)] + [pltpu.VMEM((EARLY * YD, XD), f32)] * 2,
    )(cells, weights, bias, ids, slots)
    taps, logits, early = held(taps), held(logits), held(early)
    inner, outer, own = pl.pallas_call(
        columns_kernel,
        out_shape=(near((1, WIDE), f32),) * 3,
        in_specs=whole(5),
        out_specs=tuple(whole(3)),
        scratch_shapes=[pltpu.VMEM((WIDE, XD), bf16)],
    )(two, one, cells, ids, early)
    outer = swapped(outer, "gz", 1)
    inner = swapped(inner, "gz", 0)
    logits, sums, ends = pl.pallas_call(
        inner_kernel,
        out_shape=(near((PART, XD), f32), sums_shape, near((8, 4 * XD), f32)),
        in_specs=whole(7),
        out_specs=tuple(whole(3)),
        scratch_shapes=[pltpu.VMEM((LANES, XD), bf16)] + pairs,
    )(two, one, taps, logits, early, ids, slots)
    logits = held(logits)
    outgoing = pl.pallas_call(
        send_kernel,
        out_shape=near((devices, 2 * BUCKET), f32),
        in_specs=whole(7),
        out_specs=whole(1)[0],
    )(outer, inner, taps, held(own), held(ends), held(sums), bucket)
    arrived = lax.all_to_all(held(outgoing), ("gz", "yx"), split_axis=0, concat_axis=0, tiled=True)
    affinity = pl.pallas_call(
        affinity_kernel,
        out_shape=jax.ShapeDtypeStruct((PART, XD), bf16),
        in_specs=whole(4),
        out_specs=whole(1)[0],
    )(outer, inner, taps, logits)
    mean = pl.pallas_call(
        edges_kernel,
        out_shape=jax.ShapeDtypeStruct((HIGH, LANES), f32),
        in_specs=whole(2),
        out_specs=whole(1)[0],
    )(held(arrived), targets)
    return affinity.reshape(C_OUT, Z, YD, XD), mean.reshape(E_OWN)


def solution(mesh):
    return jax.shard_map(
        local,
        mesh=mesh,
        in_specs=(
            P(None, None, "yx", "gz"),
            P(),
            P(),
            P(None, "yx", "gz"),
            P(None, None, "yx", "gz"),
            P(("gz", "yx"), None),
            P(("gz", "yx"), None, None),
        ),
        out_specs=(P(None, None, "yx", "gz"), P(("gz", "yx"))),
        check_vma=False,
    )
```

```python
import functools

import jax
import jax.numpy as jnp
from jax import lax
from jax.experimental import pallas as pl
from jax.experimental.pallas import tpu as pltpu
from jax.sharding import PartitionSpec as P

C_IN, C_OUT, Z, YD, XD = 12, 3, 4, 16, 256
BUCKET, E_OWN, P_LOC = 64, 4096, 4096
CZ = C_IN * Z
CELLS = CZ * YD
DEPTH = CELLS + 2 * CZ + 32
WIDE = DEPTH + 2 * Z * YD
ROWS = Z * YD
LANES = 128
HIGH = P_LOC // LANES

TAP_ROWS = 9 * ROWS
PART = C_OUT * ROWS
EARLY = 9
BATCH = 48
LOW, HALF, STEP = 96, 48, 12

f32, bf16, i32 = jnp.float32, jnp.bfloat16, jnp.int32


def iota(shape, dim):
    return lax.broadcasted_iota(i32, shape, dim)


def along(a, b):
    return lax.dot_general(a, b, (((1,), (1,)), ((), ())), preferred_element_type=f32)


def whole(count):
    return [pl.BlockSpec(memory_space=pltpu.VMEM)] * count


def near(shape, dtype):
    return pltpu.VMEM(shape, dtype)


def held(x):
    return pltpu.with_memory_space_constraint(x, pltpu.VMEM)


def even(axis):
    return lax.rem(lax.axis_index(axis), 2) == 0


def rows_kernel(*refs):
    count = len(refs) // 2 - 1
    sources, (one, two), held_refs, sems = refs[:count], refs[count : count + 2], refs[count + 2 : -1], refs[-1]
    copies = [pltpu.make_async_copy(a, b, sems.at[i]) for i, (a, b) in enumerate(zip(sources, held_refs))]
    for copy in copies:
        copy.start()
    cells, ids = held_refs[:2]
    row = iota((2 * CZ, CELLS), 0)
    inner = jnp.where(even("yx"), YD - 1, 0)
    wanted = jnp.where(row < CZ, row * YD + inner, (row - CZ) * YD + (YD - 1 - inner))
    pick = jnp.where(iota((2 * CZ, CELLS), 1) == wanted, 1.0, 0.0).astype(bf16)
    copies[0].wait()
    picked = jnp.dot(pick, cells[...], preferred_element_type=f32).astype(bf16)
    copies[1].wait()
    last = jnp.concatenate([ids[(z + 1) * YD - 1 : (z + 1) * YD] for z in range(Z)], axis=0)
    pair = jnp.concatenate([last >> 7, last & 127], axis=0).astype(f32).astype(bf16)
    one[:CZ] = picked[:CZ]
    two[:CZ] = picked[CZ:]
    one[CZ:] = pair
    two[CZ:] = pair
    for copy in copies[2:]:
        copy.wait()


def placed(inner, outer, axis):
    at, last, first = lax.axis_index(axis), lax.axis_size(axis) - 1, even(axis)
    before, after = jnp.where(first, outer, inner), jnp.where(first, inner, outer)
    zero = jnp.zeros((), before.dtype)
    return jnp.where(at == 0, zero, before), jnp.where(at == last, zero, after)


def pick_ends():
    row, lane = iota((8, XD), 0), iota((8, XD), 1)
    return jnp.where((row < 2) & (lane == row * (XD - 1)), 1.0, 0.0).astype(bf16)


def columns_kernel(two, one, cells, ids, after, inner, outer, own, wide):
    top, bottom = placed(one[:CZ], two[:CZ], "yx")
    wide[:CELLS] = cells[...]
    wide[CELLS : CELLS + CZ] = top
    wide[CELLS + CZ : CELLS + 2 * CZ] = bottom
    wide[CELLS + 2 * CZ : DEPTH] = jnp.zeros((DEPTH - CELLS - 2 * CZ, XD), bf16)
    wide[DEPTH : DEPTH + ROWS] = (ids[...] >> 7).astype(f32).astype(bf16)
    wide[DEPTH + ROWS :] = (ids[...] & 127).astype(f32).astype(bf16)
    picked = along(pick_ends(), wide[...])
    first = even("gz")
    inner[...] = jnp.where(first, picked[1:2], picked[0:1])
    outer[...] = jnp.where(first, picked[0:1], picked[1:2])
    own[...] = picked[0:1]


def taps_kernel(cells, weights, bias, ids, slots, taps, logits, sums, flat, value, cross):
    flat[...] = jnp.zeros(flat.shape, f32)
    for i in range(27):
        flat[8 * i : 8 * i + 3, :C_IN] = weights[i].astype(f32)
    k = iota((LANES, DEPTH), 1)
    channel = jnp.where(k < CELLS, k // (Z * YD), ((k - CELLS) % CZ) // Z)
    channel = jnp.where(k < CELLS + 2 * CZ, channel, LANES)
    spread = jnp.where(iota((LANES, DEPTH), 0) == channel, 1.0, 0.0).astype(bf16)
    lines = jnp.dot(flat[...].astype(bf16), spread, preferred_element_type=f32).astype(bf16)
    for t in range(DEPTH // LANES):
        y, k = iota((YD, LANES), 0), iota((YD, LANES), 1) + t * LANES
        inner = k < CELLS
        z_in = small(jnp.where(inner, (k // YD) % Z, (k - CELLS) % Z))
        y_in = jnp.where(inner, k % YD, jnp.where(k < CELLS + CZ, -1, YD))
        y_in = jnp.where(k < CELLS + 2 * CZ, y_in, 3 * YD)
        dy = small(y_in - y + 1)
        for e in range(3):
            for o in range(C_OUT):
                bands = []
                for a in range(3):
                    band = jnp.zeros((YD, LANES), bf16)
                    for b in range(3):
                        r = (o * 9 + a * 3 + b) * 8 + e
                        band = jnp.where(dy == float(b), lines[r : r + 1, t * LANES : (t + 1) * LANES], band)
                    bands.append(band)
                for z in range(Z):
                    tap = jnp.zeros((YD, LANES), bf16)
                    for a in range(3):
                        if 0 <= z + a - 1 < Z:
                            tap = jnp.where(z_in == float(z + a - 1), bands[a], tap)
                    row = ((e * C_OUT + o) * Z + z) * YD
                    taps[row : row + YD, t * LANES : (t + 1) * LANES] = tap
    product = jnp.dot(taps[:, :CELLS], cells[...], preferred_element_type=f32)
    offset = jnp.concatenate([jnp.broadcast_to(bias[:, o : o + 1], (ROWS, 1)) for o in range(C_OUT)], axis=0)
    total = shifted(product) + offset
    logits[...] = total
    rows = EARLY * YD
    fill_pairs(total[:rows], crossings(ids[...], None)[:rows], value, cross)
    sums[...] = batched([line for i in range(1, EARLY) for line in lines_of(i, range(1, YD - 1), slots, value, cross)])


def shifted(product):
    lane = iota((PART, XD), 1)
    total = product[PART : 2 * PART]
    total += jnp.where(lane == 0, 0.0, pltpu.roll(product[:PART], 1, 1))
    return total + jnp.where(lane == XD - 1, 0.0, pltpu.roll(product[2 * PART :], XD - 1, 1))


def sigmoid(x):
    return (1.0 / (1.0 + jnp.exp(-x))).astype(bf16)


def one_hot(line, count, value=None):
    rows = iota((count, line.shape[1]), 0).astype(f32).astype(bf16)
    return jnp.where(rows == line, jnp.ones((), bf16) if value is None else value, jnp.zeros((), bf16))


def pair_hot(line, count, first, second):
    return jnp.concatenate([one_hot(line, count, first), one_hot(line, count, second)], axis=0)


def small(x):
    return x.astype(f32).astype(bf16)


def split(number):
    q = ((number >> 5) * 171) >> 9
    return small((q & 3) * STEP + (q >> 2)), small(number - q * LOW)


def chunk_sums(chunks):
    a_parts = [pair_hot(row, HALF, value, cross) for row, _, value, cross in chunks]
    b_parts = [one_hot(column, LOW) for _, column, _, _ in chunks]
    return along(jnp.concatenate(a_parts, axis=1), jnp.concatenate(b_parts, axis=1))


def relaid(total):
    a, b, c, d = (total[j * STEP : (j + 1) * STEP] for j in range(4))
    return (
        jnp.concatenate([a, b[:, :32]], axis=1),
        jnp.concatenate([b[:, 32:], c[:, :64]], axis=1),
        jnp.concatenate([c[:, 64:], d], axis=1),
    )


def crossings(here, above):
    m, n = iota((ROWS, XD), 0), iota((ROWS, XD), 1)
    under_z = jnp.concatenate([here[:YD], here[:-YD]], axis=0)
    under_y = pltpu.roll(here, 1, 0)
    if above is not None:
        above = jnp.concatenate([jnp.broadcast_to(above[z : z + 1], (YD, XD)) for z in range(Z)], axis=0)
        under_y = jnp.where(m % YD == 0, above, under_y)
    under_x = jnp.where(n == 0, here, pltpu.roll(here, 1, 1))
    unders = (under_z, under_y, under_x)
    return jnp.concatenate([jnp.where((here != under) & (under > 0), 1.0, 0.0) for under in unders], axis=0)


def fill_pairs(logits, crossed, value, cross):
    n = iota(logits.shape, 1)
    crossed = jnp.where((n > 0) & (n < XD - 1), crossed, 0.0)
    cross[...] = crossed
    value[...] = crossed * sigmoid(logits).astype(f32)


def lines_of(i, rows, slots, value, cross):
    at = slice(i * YD, (i + 1) * YD)
    tiles = (*split(slots[at]), value[at].astype(bf16), cross[at].astype(bf16))
    return [[tile[j : j + 1] for tile in tiles] for j in rows]


def batched(chunks, size=BATCH):
    return sum(chunk_sums(chunks[i : i + size]) for i in range(0, len(chunks), size))


def inner_kernel(two, one, taps, logits, early, ids, slots, full, sums, ends, halo, value, cross):
    top, bottom = placed(one[...].astype(f32), two[...].astype(f32), "yx")
    halo[:CZ] = top[:CZ].astype(bf16)
    halo[CZ : 2 * CZ] = bottom[:CZ].astype(bf16)
    halo[2 * CZ :] = jnp.zeros((LANES - 2 * CZ, XD), bf16)
    total = logits[...] + shifted(jnp.dot(taps[:, CELLS:], halo[...], preferred_element_type=f32))
    full[...] = total
    above = top[CZ:]
    above = (above[:Z] * 128.0 + above[Z:]).astype(i32)
    crossed = crossings(ids[...], above)
    fill_pairs(total, crossed, value, cross)
    pad = jnp.zeros((XD - PART, XD), f32)
    numbers = slots[...]
    kinds = [crossed, (numbers >> 7).astype(f32), (numbers & 127).astype(f32)]
    rest = total
    for _ in range(3):
        kinds.append(rest.astype(bf16).astype(f32))
        rest = rest - kinds[-1]
    kinds = jnp.concatenate([part for kind in kinds for part in (kind, pad)], axis=0)
    picked = along(pick_ends(), kinds.astype(bf16))
    ends[:, : 3 * XD] = picked[:, : 3 * XD]
    ends[:, 3 * XD :] = picked[:, 3 * XD : 4 * XD] + picked[:, 4 * XD : 5 * XD] + picked[:, 5 * XD :]
    chunks = [line for i in range(1, EARLY) for line in lines_of(i, (0, YD - 1), slots, value, cross)]
    chunks += [line for i in range(EARLY, C_OUT * Z) for line in lines_of(i, range(YD), slots, value, cross)]
    sums[...] = early[...] + batched(chunks)


def end_rows(left, right):
    row = iota((8, DEPTH), 0)
    return jnp.where(row == 0, left[:, :DEPTH], jnp.where(row == 1, right[:, :DEPTH], 0.0)).astype(bf16)


def send_kernel(outer, inner, taps, own, ends, sums, bucket, outgoing):
    left, right = placed(inner[...], outer[...], "gz")
    both = end_rows(left, right)
    first = along(both, taps[:PART])[0:1] + ends[0:1, 3 * XD : 3 * XD + PART]
    last = along(both, taps[2 * PART :])[1:2] + ends[1:2, 3 * XD : 3 * XD + PART]
    soft = sigmoid(jnp.concatenate([first, last], axis=0)).astype(f32)
    soft = jnp.concatenate([soft, jnp.zeros((2, XD - PART), f32)], axis=1)

    beside = left[:, DEPTH : DEPTH + ROWS] * 128.0 + left[:, DEPTH + ROWS :]
    here = own[:, DEPTH : DEPTH + ROWS] * 128.0 + own[:, DEPTH + ROWS :]
    differs = jnp.where((beside != here) & (beside > 0.0), 1.0, 0.0)
    differs = jnp.concatenate([jnp.zeros((1, 2 * ROWS), f32), differs, jnp.zeros((1, XD - PART), f32)], axis=1)
    chunks = []
    for end in range(2):
        crossed = ends[end : end + 1, :XD]
        if end == 0:
            crossed = crossed + differs
        slot = ends[end : end + 1, XD : 2 * XD] * 128.0 + ends[end : end + 1, 2 * XD : 3 * XD]
        chunks.append((*split(slot.astype(i32)), (soft[end : end + 1] * crossed).astype(bf16), crossed.astype(bf16)))
    total = sums[...] + chunk_sums(chunks)
    kinds = [[part.astype(bf16) for part in relaid(total[at : at + HALF])] for at in (0, HALF)]
    owners, places = small(bucket[...] >> 6), small(bucket[...] & 63)
    a_parts, b_parts = [], []
    for h in range(HIGH):
        k, j = divmod(h, 3)
        a_parts.append(one_hot(owners[h : h + 1], LANES))
        b_parts.append(pair_hot(places[h : h + 1], BUCKET, kinds[0][j][k : k + 1], kinds[1][j][k : k + 1]))
    sent = along(jnp.concatenate(a_parts, axis=1), jnp.concatenate(b_parts, axis=1))
    outgoing[...] = sent


def affinity_kernel(outer, inner, taps, logits, affinity):
    both = end_rows(*placed(inner[...], outer[...], "gz"))
    first = along(taps[:PART], both)[:, 0:1]
    last = along(taps[2 * PART :], both)[:, 1:2]
    lane = iota((PART, XD), 1)
    ends = jnp.where(lane == 0, first, jnp.where(lane == XD - 1, last, 0.0))
    affinity[...] = sigmoid(logits[...] + ends)


def edges_kernel(arrived, rows, mean):
    got = arrived[...].T.astype(bf16)
    row, column = split(rows[...])
    total = chunk_sums(
        [
            (row[q : q + 1], column[q : q + 1], got[q : q + 1], got[BUCKET + q : BUCKET + q + 1])
            for q in range(BUCKET)
        ]
    )
    parts = relaid(total[:HALF] / jnp.maximum(total[HALF:], 1.0))
    for h in range(HIGH):
        k, j = divmod(h, 3)
        mean[h : h + 1] = parts[j][k : k + 1]


def swapped(block, axis, first):
    gz, yx = lax.axis_size("gz"), lax.axis_size("yx")
    pairs = []
    for g in range(gz):
        for y in range(yx):
            at, size = (g, gz) if axis == "gz" else (y, yx)
            to = at + 1 if (at - first) % 2 == 0 else at - 1
            if not 0 <= to < size:
                g_to, y_to = (g, y ^ 1) if axis == "gz" else (g ^ 1, y)
            else:
                g_to, y_to = (to, y) if axis == "gz" else (g, to)
            pairs.append((g * yx + y, g_to * yx + y_to))
    return held(lax.ppermute(block, ("gz", "yx"), pairs))


def local(features, conv_weight, conv_bias, fragments, pair_slot, slot_bucket, arrival_row):
    devices = lax.axis_size("gz") * lax.axis_size("yx")
    inputs = (
        features.reshape(CELLS, XD),
        fragments.reshape(ROWS, XD),
        pair_slot.reshape(PART, XD),
        conv_weight.transpose(0, 2, 3, 4, 1).reshape(27, 3, C_IN),
        slot_bucket.reshape(HIGH, LANES),
        arrival_row[0].T,
        conv_bias.reshape(1, C_OUT),
    )
    pairs = [pltpu.VMEM((PART, XD), f32)] * 2
    sums_shape = near((2 * HALF, LOW), f32)
    lines = near((CZ + 2 * Z, XD), bf16)
    one, two, *inputs = pl.pallas_call(
        rows_kernel,
        out_shape=(lines, lines, *(near(x.shape, x.dtype) for x in inputs)),
        in_specs=[pl.BlockSpec(memory_space=pl.ANY)] * len(inputs),
        out_specs=tuple(whole(2 + len(inputs))),
        scratch_shapes=[pltpu.SemaphoreType.DMA((len(inputs),))],
    )(*inputs)
    cells, ids, slots, weights, bucket, targets, bias = map(held, inputs)
    two = swapped(two, "yx", 1)
    one = swapped(one, "yx", 0)
    taps, logits, early = pl.pallas_call(
        taps_kernel,
        out_shape=(near((TAP_ROWS, DEPTH), bf16), near((PART, XD), f32), sums_shape),
        in_specs=whole(5),
        out_specs=tuple(whole(3)),
        scratch_shapes=[pltpu.VMEM((27 * 8, LANES), f32)] + [pltpu.VMEM((EARLY * YD, XD), f32)] * 2,
    )(cells, weights, bias, ids, slots)
    taps, logits, early = held(taps), held(logits), held(early)
    inner, outer, own = pl.pallas_call(
        columns_kernel,
        out_shape=(near((1, WIDE), f32),) * 3,
        in_specs=whole(5),
        out_specs=tuple(whole(3)),
        scratch_shapes=[pltpu.VMEM((WIDE, XD), bf16)],
    )(two, one, cells, ids, early)
    outer = swapped(outer, "gz", 1)
    inner = swapped(inner, "gz", 0)
    logits, sums, ends = pl.pallas_call(
        inner_kernel,
        out_shape=(near((PART, XD), f32), sums_shape, near((8, 4 * XD), f32)),
        in_specs=whole(7),
        out_specs=tuple(whole(3)),
        scratch_shapes=[pltpu.VMEM((LANES, XD), bf16)] + pairs,
    )(two, one, taps, logits, early, ids, slots)
    logits = held(logits)
    outgoing = pl.pallas_call(
        send_kernel,
        out_shape=near((devices, 2 * BUCKET), f32),
        in_specs=whole(7),
        out_specs=whole(1)[0],
    )(outer, inner, taps, held(own), held(ends), held(sums), bucket)
    arrived = lax.all_to_all(held(outgoing), ("gz", "yx"), split_axis=0, concat_axis=0, tiled=True)
    affinity = pl.pallas_call(
        affinity_kernel,
        out_shape=jax.ShapeDtypeStruct((PART, XD), bf16),
        in_specs=whole(4),
        out_specs=whole(1)[0],
    )(outer, inner, taps, logits)
    mean = pl.pallas_call(
        edges_kernel,
        out_shape=jax.ShapeDtypeStruct((HIGH, LANES), f32),
        in_specs=whole(2),
        out_specs=whole(1)[0],
    )(held(arrived), targets)
    return affinity.reshape(C_OUT, Z, YD, XD), mean.reshape(E_OWN)


def solution(mesh):
    return jax.shard_map(
        local,
        mesh=mesh,
        in_specs=(
            P(None, None, "yx", "gz"),
            P(),
            P(),
            P(None, "yx", "gz"),
            P(None, None, "yx", "gz"),
            P(("gz", "yx"), None),
            P(("gz", "yx"), None, None),
        ),
        out_specs=(P(None, None, "yx", "gz"), P(("gz", "yx"))),
        check_vma=False,
    )
```

```python
import functools

import jax
import jax.numpy as jnp
from jax import lax
from jax.experimental import pallas as pl
from jax.experimental.pallas import tpu as pltpu
from jax.sharding import PartitionSpec as P

C_IN, C_OUT, Z, YD, XD = 12, 3, 4, 16, 256
BUCKET, E_OWN, P_LOC = 64, 4096, 4096
CZ = C_IN * Z
CELLS = CZ * YD
DEPTH = CELLS + 2 * CZ + 32
WIDE = DEPTH + 2 * Z * YD
ROWS = Z * YD
LANES = 128
HIGH = P_LOC // LANES

TAP_ROWS = 9 * ROWS
PART = C_OUT * ROWS
EARLY = 9
BATCH = 128
LOW, HALF, STEP = 96, 48, 12

f32, bf16, i32 = jnp.float32, jnp.bfloat16, jnp.int32


def iota(shape, dim):
    return lax.broadcasted_iota(i32, shape, dim)


def along(a, b):
    return lax.dot_general(a, b, (((1,), (1,)), ((), ())), preferred_element_type=f32)


def whole(count):
    return [pl.BlockSpec(memory_space=pltpu.VMEM)] * count


def near(shape, dtype):
    return pltpu.VMEM(shape, dtype)


def held(x):
    return pltpu.with_memory_space_constraint(x, pltpu.VMEM)


def even(axis):
    return lax.rem(lax.axis_index(axis), 2) == 0


def rows_kernel(*refs):
    count = len(refs) // 2 - 1
    sources, (one, two), held_refs, sems = refs[:count], refs[count : count + 2], refs[count + 2 : -1], refs[-1]
    copies = [pltpu.make_async_copy(a, b, sems.at[i]) for i, (a, b) in enumerate(zip(sources, held_refs))]
    for copy in copies:
        copy.start()
    cells, ids = held_refs[:2]
    row = iota((2 * CZ, CELLS), 0)
    inner = jnp.where(even("yx"), YD - 1, 0)
    wanted = jnp.where(row < CZ, row * YD + inner, (row - CZ) * YD + (YD - 1 - inner))
    pick = jnp.where(iota((2 * CZ, CELLS), 1) == wanted, 1.0, 0.0).astype(bf16)
    copies[0].wait()
    picked = jnp.dot(pick, cells[...], preferred_element_type=f32).astype(bf16)
    copies[1].wait()
    last = jnp.concatenate([ids[(z + 1) * YD - 1 : (z + 1) * YD] for z in range(Z)], axis=0)
    pair = jnp.concatenate([last >> 7, last & 127], axis=0).astype(f32).astype(bf16)
    one[:CZ] = picked[:CZ]
    two[:CZ] = picked[CZ:]
    one[CZ:] = pair
    two[CZ:] = pair
    for copy in copies[2:]:
        copy.wait()


def placed(inner, outer, axis):
    at, last, first = lax.axis_index(axis), lax.axis_size(axis) - 1, even(axis)
    before, after = jnp.where(first, outer, inner), jnp.where(first, inner, outer)
    zero = jnp.zeros((), before.dtype)
    return jnp.where(at == 0, zero, before), jnp.where(at == last, zero, after)


def pick_ends():
    row, lane = iota((8, XD), 0), iota((8, XD), 1)
    return jnp.where((row < 2) & (lane == row * (XD - 1)), 1.0, 0.0).astype(bf16)


def columns_kernel(two, one, cells, ids, after, inner, outer, own, wide):
    top, bottom = placed(one[:CZ], two[:CZ], "yx")
    wide[:CELLS] = cells[...]
    wide[CELLS : CELLS + CZ] = top
    wide[CELLS + CZ : CELLS + 2 * CZ] = bottom
    wide[CELLS + 2 * CZ : DEPTH] = jnp.zeros((DEPTH - CELLS - 2 * CZ, XD), bf16)
    wide[DEPTH : DEPTH + ROWS] = (ids[...] >> 7).astype(f32).astype(bf16)
    wide[DEPTH + ROWS :] = (ids[...] & 127).astype(f32).astype(bf16)
    picked = along(pick_ends(), wide[...])
    first = even("gz")
    inner[...] = jnp.where(first, picked[1:2], picked[0:1])
    outer[...] = jnp.where(first, picked[0:1], picked[1:2])
    own[...] = picked[0:1]


def taps_kernel(cells, weights, bias, ids, slots, taps, logits, sums, flat, value, cross):
    flat[...] = jnp.zeros(flat.shape, f32)
    for i in range(27):
        flat[8 * i : 8 * i + 3, :C_IN] = weights[i].astype(f32)
    k = iota((LANES, DEPTH), 1)
    channel = jnp.where(k < CELLS, k // (Z * YD), ((k - CELLS) % CZ) // Z)
    channel = jnp.where(k < CELLS + 2 * CZ, channel, LANES)
    spread = jnp.where(iota((LANES, DEPTH), 0) == channel, 1.0, 0.0).astype(bf16)
    lines = jnp.dot(flat[...].astype(bf16), spread, preferred_element_type=f32).astype(bf16)
    for t in range(DEPTH // LANES):
        y, k = iota((YD, LANES), 0), iota((YD, LANES), 1) + t * LANES
        inner = k < CELLS
        z_in = small(jnp.where(inner, (k // YD) % Z, (k - CELLS) % Z))
        y_in = jnp.where(inner, k % YD, jnp.where(k < CELLS + CZ, -1, YD))
        y_in = jnp.where(k < CELLS + 2 * CZ, y_in, 3 * YD)
        dy = small(y_in - y + 1)
        for e in range(3):
            for o in range(C_OUT):
                bands = []
                for a in range(3):
                    band = jnp.zeros((YD, LANES), bf16)
                    for b in range(3):
                        r = (o * 9 + a * 3 + b) * 8 + e
                        band = jnp.where(dy == float(b), lines[r : r + 1, t * LANES : (t + 1) * LANES], band)
                    bands.append(band)
                for z in range(Z):
                    tap = jnp.zeros((YD, LANES), bf16)
                    for a in range(3):
                        if 0 <= z + a - 1 < Z:
                            tap = jnp.where(z_in == float(z + a - 1), bands[a], tap)
                    row = ((e * C_OUT + o) * Z + z) * YD
                    taps[row : row + YD, t * LANES : (t + 1) * LANES] = tap
    product = jnp.dot(taps[:, :CELLS], cells[...], preferred_element_type=f32)
    offset = jnp.concatenate([jnp.broadcast_to(bias[:, o : o + 1], (ROWS, 1)) for o in range(C_OUT)], axis=0)
    total = shifted(product) + offset
    logits[...] = total
    rows = EARLY * YD
    fill_pairs(total[:rows], crossings(ids[...], None)[:rows], value, cross)
    sums[...] = batched([line for i in range(1, EARLY) for line in lines_of(i, range(1, YD - 1), slots, value, cross)])


def shifted(product):
    lane = iota((PART, XD), 1)
    total = product[PART : 2 * PART]
    total += jnp.where(lane == 0, 0.0, pltpu.roll(product[:PART], 1, 1))
    return total + jnp.where(lane == XD - 1, 0.0, pltpu.roll(product[2 * PART :], XD - 1, 1))


def sigmoid(x):
    return (1.0 / (1.0 + jnp.exp(-x))).astype(bf16)


def one_hot(line, count, value=None):
    rows = iota((count, line.shape[1]), 0).astype(f32).astype(bf16)
    return jnp.where(rows == line, jnp.ones((), bf16) if value is None else value, jnp.zeros((), bf16))


def pair_hot(line, count, first, second):
    return jnp.concatenate([one_hot(line, count, first), one_hot(line, count, second)], axis=0)


def small(x):
    return x.astype(f32).astype(bf16)


def split(number):
    q = ((number >> 5) * 171) >> 9
    return small((q & 3) * STEP + (q >> 2)), small(number - q * LOW)


def chunk_sums(chunks):
    a_parts = [pair_hot(row, HALF, value, cross) for row, _, value, cross in chunks]
    b_parts = [one_hot(column, LOW) for _, column, _, _ in chunks]
    return along(jnp.concatenate(a_parts, axis=1), jnp.concatenate(b_parts, axis=1))


def relaid(total):
    a, b, c, d = (total[j * STEP : (j + 1) * STEP] for j in range(4))
    return (
        jnp.concatenate([a, b[:, :32]], axis=1),
        jnp.concatenate([b[:, 32:], c[:, :64]], axis=1),
        jnp.concatenate([c[:, 64:], d], axis=1),
    )


def crossings(here, above):
    m, n = iota((ROWS, XD), 0), iota((ROWS, XD), 1)
    under_z = jnp.concatenate([here[:YD], here[:-YD]], axis=0)
    under_y = pltpu.roll(here, 1, 0)
    if above is not None:
        above = jnp.concatenate([jnp.broadcast_to(above[z : z + 1], (YD, XD)) for z in range(Z)], axis=0)
        under_y = jnp.where(m % YD == 0, above, under_y)
    under_x = jnp.where(n == 0, here, pltpu.roll(here, 1, 1))
    unders = (under_z, under_y, under_x)
    return jnp.concatenate([jnp.where((here != under) & (under > 0), 1.0, 0.0) for under in unders], axis=0)


def fill_pairs(logits, crossed, value, cross):
    n = iota(logits.shape, 1)
    crossed = jnp.where((n > 0) & (n < XD - 1), crossed, 0.0)
    cross[...] = crossed
    value[...] = crossed * sigmoid(logits).astype(f32)


def lines_of(i, rows, slots, value, cross):
    at = slice(i * YD, (i + 1) * YD)
    tiles = (*split(slots[at]), value[at].astype(bf16), cross[at].astype(bf16))
    return [[tile[j : j + 1] for tile in tiles] for j in rows]


def batched(chunks, size=BATCH):
    return sum(chunk_sums(chunks[i : i + size]) for i in range(0, len(chunks), size))


def inner_kernel(two, one, taps, logits, early, ids, slots, full, sums, ends, halo, value, cross):
    top, bottom = placed(one[...].astype(f32), two[...].astype(f32), "yx")
    halo[:CZ] = top[:CZ].astype(bf16)
    halo[CZ : 2 * CZ] = bottom[:CZ].astype(bf16)
    halo[2 * CZ :] = jnp.zeros((LANES - 2 * CZ, XD), bf16)
    total = logits[...] + shifted(jnp.dot(taps[:, CELLS:], halo[...], preferred_element_type=f32))
    full[...] = total
    above = top[CZ:]
    above = (above[:Z] * 128.0 + above[Z:]).astype(i32)
    crossed = crossings(ids[...], above)
    fill_pairs(total, crossed, value, cross)
    pad = jnp.zeros((XD - PART, XD), f32)
    numbers = slots[...]
    kinds = [crossed, (numbers >> 7).astype(f32), (numbers & 127).astype(f32)]
    rest = total
    for _ in range(3):
        kinds.append(rest.astype(bf16).astype(f32))
        rest = rest - kinds[-1]
    kinds = jnp.concatenate([part for kind in kinds for part in (kind, pad)], axis=0)
    picked = along(pick_ends(), kinds.astype(bf16))
    ends[:, : 3 * XD] = picked[:, : 3 * XD]
    ends[:, 3 * XD :] = picked[:, 3 * XD : 4 * XD] + picked[:, 4 * XD : 5 * XD] + picked[:, 5 * XD :]
    chunks = [line for i in range(1, EARLY) for line in lines_of(i, (0, YD - 1), slots, value, cross)]
    chunks += [line for i in range(EARLY, C_OUT * Z) for line in lines_of(i, range(YD), slots, value, cross)]
    sums[...] = early[...] + batched(chunks)


def end_rows(left, right):
    row = iota((8, DEPTH), 0)
    return jnp.where(row == 0, left[:, :DEPTH], jnp.where(row == 1, right[:, :DEPTH], 0.0)).astype(bf16)


def send_kernel(outer, inner, taps, own, ends, sums, bucket, outgoing):
    left, right = placed(inner[...], outer[...], "gz")
    both = end_rows(left, right)
    first = along(both, taps[:PART])[0:1] + ends[0:1, 3 * XD : 3 * XD + PART]
    last = along(both, taps[2 * PART :])[1:2] + ends[1:2, 3 * XD : 3 * XD + PART]
    soft = sigmoid(jnp.concatenate([first, last], axis=0)).astype(f32)
    soft = jnp.concatenate([soft, jnp.zeros((2, XD - PART), f32)], axis=1)

    beside = left[:, DEPTH : DEPTH + ROWS] * 128.0 + left[:, DEPTH + ROWS :]
    here = own[:, DEPTH : DEPTH + ROWS] * 128.0 + own[:, DEPTH + ROWS :]
    differs = jnp.where((beside != here) & (beside > 0.0), 1.0, 0.0)
    differs = jnp.concatenate([jnp.zeros((1, 2 * ROWS), f32), differs, jnp.zeros((1, XD - PART), f32)], axis=1)
    chunks = []
    for end in range(2):
        crossed = ends[end : end + 1, :XD]
        if end == 0:
            crossed = crossed + differs
        slot = ends[end : end + 1, XD : 2 * XD] * 128.0 + ends[end : end + 1, 2 * XD : 3 * XD]
        chunks.append((*split(slot.astype(i32)), (soft[end : end + 1] * crossed).astype(bf16), crossed.astype(bf16)))
    total = sums[...] + chunk_sums(chunks)
    kinds = [[part.astype(bf16) for part in relaid(total[at : at + HALF])] for at in (0, HALF)]
    owners, places = small(bucket[...] >> 6), small(bucket[...] & 63)
    a_parts, b_parts = [], []
    for h in range(HIGH):
        k, j = divmod(h, 3)
        a_parts.append(one_hot(owners[h : h + 1], LANES))
        b_parts.append(pair_hot(places[h : h + 1], BUCKET, kinds[0][j][k : k + 1], kinds[1][j][k : k + 1]))
    sent = along(jnp.concatenate(a_parts, axis=1), jnp.concatenate(b_parts, axis=1))
    outgoing[...] = sent


def affinity_kernel(outer, inner, taps, logits, affinity):
    both = end_rows(*placed(inner[...], outer[...], "gz"))
    first = along(taps[:PART], both)[:, 0:1]
    last = along(taps[2 * PART :], both)[:, 1:2]
    lane = iota((PART, XD), 1)
    ends = jnp.where(lane == 0, first, jnp.where(lane == XD - 1, last, 0.0))
    affinity[...] = sigmoid(logits[...] + ends)


def edges_kernel(arrived, rows, mean):
    got = arrived[...].T.astype(bf16)
    row, column = split(rows[...])
    total = chunk_sums(
        [
            (row[q : q + 1], column[q : q + 1], got[q : q + 1], got[BUCKET + q : BUCKET + q + 1])
            for q in range(BUCKET)
        ]
    )
    parts = relaid(total[:HALF] / jnp.maximum(total[HALF:], 1.0))
    for h in range(HIGH):
        k, j = divmod(h, 3)
        mean[h : h + 1] = parts[j][k : k + 1]


def swapped(block, axis, first):
    gz, yx = lax.axis_size("gz"), lax.axis_size("yx")
    pairs = []
    for g in range(gz):
        for y in range(yx):
            at, size = (g, gz) if axis == "gz" else (y, yx)
            to = at + 1 if (at - first) % 2 == 0 else at - 1
            if not 0 <= to < size:
                g_to, y_to = (g, y ^ 1) if axis == "gz" else (g ^ 1, y)
            else:
                g_to, y_to = (to, y) if axis == "gz" else (g, to)
            pairs.append((g * yx + y, g_to * yx + y_to))
    return held(lax.ppermute(block, ("gz", "yx"), pairs))


def local(features, conv_weight, conv_bias, fragments, pair_slot, slot_bucket, arrival_row):
    devices = lax.axis_size("gz") * lax.axis_size("yx")
    inputs = (
        features.reshape(CELLS, XD),
        fragments.reshape(ROWS, XD),
        pair_slot.reshape(PART, XD),
        conv_weight.transpose(0, 2, 3, 4, 1).reshape(27, 3, C_IN),
        slot_bucket.reshape(HIGH, LANES),
        arrival_row[0].T,
        conv_bias.reshape(1, C_OUT),
    )
    pairs = [pltpu.VMEM((PART, XD), f32)] * 2
    sums_shape = near((2 * HALF, LOW), f32)
    lines = near((CZ + 2 * Z, XD), bf16)
    one, two, *inputs = pl.pallas_call(
        rows_kernel,
        out_shape=(lines, lines, *(near(x.shape, x.dtype) for x in inputs)),
        in_specs=[pl.BlockSpec(memory_space=pl.ANY)] * len(inputs),
        out_specs=tuple(whole(2 + len(inputs))),
        scratch_shapes=[pltpu.SemaphoreType.DMA((len(inputs),))],
    )(*inputs)
    cells, ids, slots, weights, bucket, targets, bias = map(held, inputs)
    two = swapped(two, "yx", 1)
    one = swapped(one, "yx", 0)
    taps, logits, early = pl.pallas_call(
        taps_kernel,
        out_shape=(near((TAP_ROWS, DEPTH), bf16), near((PART, XD), f32), sums_shape),
        in_specs=whole(5),
        out_specs=tuple(whole(3)),
        scratch_shapes=[pltpu.VMEM((27 * 8, LANES), f32)] + [pltpu.VMEM((EARLY * YD, XD), f32)] * 2,
    )(cells, weights, bias, ids, slots)
    taps, logits, early = held(taps), held(logits), held(early)
    inner, outer, own = pl.pallas_call(
        columns_kernel,
        out_shape=(near((1, WIDE), f32),) * 3,
        in_specs=whole(5),
        out_specs=tuple(whole(3)),
        scratch_shapes=[pltpu.VMEM((WIDE, XD), bf16)],
    )(two, one, cells, ids, early)
    outer = swapped(outer, "gz", 1)
    inner = swapped(inner, "gz", 0)
    logits, sums, ends = pl.pallas_call(
        inner_kernel,
        out_shape=(near((PART, XD), f32), sums_shape, near((8, 4 * XD), f32)),
        in_specs=whole(7),
        out_specs=tuple(whole(3)),
        scratch_shapes=[pltpu.VMEM((LANES, XD), bf16)] + pairs,
    )(two, one, taps, logits, early, ids, slots)
    logits = held(logits)
    outgoing = pl.pallas_call(
        send_kernel,
        out_shape=near((devices, 2 * BUCKET), f32),
        in_specs=whole(7),
        out_specs=whole(1)[0],
    )(outer, inner, taps, held(own), held(ends), held(sums), bucket)
    arrived = lax.all_to_all(held(outgoing), ("gz", "yx"), split_axis=0, concat_axis=0, tiled=True)
    affinity = pl.pallas_call(
        affinity_kernel,
        out_shape=jax.ShapeDtypeStruct((PART, XD), bf16),
        in_specs=whole(4),
        out_specs=whole(1)[0],
    )(outer, inner, taps, logits)
    mean = pl.pallas_call(
        edges_kernel,
        out_shape=jax.ShapeDtypeStruct((HIGH, LANES), f32),
        in_specs=whole(2),
        out_specs=whole(1)[0],
    )(held(arrived), targets)
    return affinity.reshape(C_OUT, Z, YD, XD), mean.reshape(E_OWN)


def solution(mesh):
    return jax.shard_map(
        local,
        mesh=mesh,
        in_specs=(
            P(None, None, "yx", "gz"),
            P(),
            P(),
            P(None, "yx", "gz"),
            P(None, None, "yx", "gz"),
            P(("gz", "yx"), None),
            P(("gz", "yx"), None, None),
        ),
        out_specs=(P(None, None, "yx", "gz"), P(("gz", "yx"))),
        check_vma=False,
    )
```
